512 devices in a mesh: sec: 128 (over y, z, core), ch: 4 (over x).
Axes of the slice: x: 4, y: 8, z: 8, core: 2. Of those that a mesh axis runs over, the one named last changes fastest.
Arguments:
- outer_wave: float32 [2, 1536, 16384], P(None, 'ch', 'sec'), may hold values from -3 to 3
- inner_wave: float32 [2, 32768], P(None, ('sec', 'ch'))
- surface: float32 [2, 32768, 1536], P(None, ('sec', 'ch'))
- energies: float32 [32768], P(('sec', 'ch')), may hold values from -2 to 100
- coefficients: float32 [12, 8, 128, 128], P('ch'), as said below
- block_cols: int32 [12, 8], replicated, may hold values from 0 to 11, as said below
- block_kind: int32 [12, 8], replicated, may hold values from 0 to 2, as said below
- polarisation: int32 [12, 8], replicated, may hold values from 0 to 2, as said below
- laser_field: float32 [3], replicated, may hold values from -0.05 to 0.05
Outputs:
- new_outer: float32 [2, 1536, 16384], P(None, 'ch', 'sec')
- new_inner: float32 [2, 32768], P(None, ('sec', 'ch'))
The draws below stay inside these ranges and needn't reach their ends.
Inputs may be any that keep to these rules, and one draw needn't show every extreme that they name: Each row of block_cols names 8 different channel blocks; block c stands in row b exactly when b stands in row c, and the two slots then carry the same kind, the same polarisation and mutually transposed coefficient blocks. `block_kind`: equal for the two slots of a mutually coupled pair of blocks. `polarisation`: equal for the two slots of a mutually coupled pair of blocks. coefficients of the slot that couples block c to block b are the transpose of those that couple b to c; a block coupled to itself has a symmetric block.
All inputs are finite; a program needn't handle non-finite values.
Results may differ from the reference program's by a relative error of at most 0.0003.
Values sent between devices are 32-bit elements; how exact they have to be, the bound alone decides.
A program may use at most 64 MiB of HBM per device.

```python
import math
import jax
import jax.numpy as jnp
from jax import lax

CHANNELS = 1536
BS = 128
SLOTS = 8
ITERS = 4
BLOCKS = 12
STATES = 32768
RADIAL = 16384


def coupling_plan(key):
    block_count = CHANNELS // BS
    labels = jax.random.permutation(jax.random.fold_in(key, 11), block_count).astype(jnp.int32)
    places = jnp.argsort(labels).astype(jnp.int32)
    positive = jax.random.permutation(jax.random.fold_in(key, 12), block_count // 2 - 1)[:(SLOTS - 2) // 2]
    positive = positive.astype(jnp.int32) + 1
    offsets = jnp.concatenate([jnp.zeros((1,), jnp.int32), positive, -positive, jnp.full((1,), block_count // 2, jnp.int32)])
    slot_order = jax.random.permutation(jax.random.fold_in(key, 13), jnp.tile(jnp.arange(SLOTS, dtype=jnp.int32), (block_count, 1)), axis=1, independent=True)
    offsets_row = offsets[slot_order]
    targets = jnp.mod(labels[:, None] + offsets_row, block_count)
    return (labels, targets, places[targets])


def pair_table(key, salt_value, top_value):
    block_count = CHANNELS // BS
    raw_table = jax.random.randint(jax.random.fold_in(key, salt_value), (block_count, block_count), 0, top_value)
    upper_mask = jnp.arange(block_count)[:, None] <= jnp.arange(block_count)[None, :]
    return jnp.where(upper_mask, raw_table, raw_table.T)


def draw_block_cols(key, part):
    labels, targets, cols_table = coupling_plan(key)
    return cols_table.astype(jnp.int32)


def draw_block_kind(key, part):
    labels, targets, cols_table = coupling_plan(key)
    return pair_table(key, 15, 3)[labels[:, None], targets].astype(jnp.int32)


def draw_polarisation(key, part):
    labels, targets, cols_table = coupling_plan(key)
    return pair_table(key, 16, 3)[labels[:, None], targets].astype(jnp.int32)


def draw_coefficients(key, part):
    block_count = CHANNELS // BS
    labels, targets, cols_table = coupling_plan(key)
    raw_table = jax.random.normal(jax.random.fold_in(key, 14), (block_count, block_count, BS, BS), jnp.float32)
    raw_table = raw_table * (1.0 / math.sqrt(BS * SLOTS))
    source_label = jnp.broadcast_to(labels[:, None], targets.shape)
    low_label = jnp.minimum(source_label, targets)
    high_label = jnp.maximum(source_label, targets)
    base_blocks = raw_table[low_label, high_label]
    flipped = jnp.swapaxes(base_blocks, -1, -2)
    symmetric = 0.5 * (base_blocks + flipped)
    below = (source_label < targets)[..., None, None]
    above = (source_label > targets)[..., None, None]
    return jnp.where(below, base_blocks, jnp.where(above, flipped, symmetric)).astype(jnp.float32)


def draw_surface(key, part):
    sign_bits = jax.random.randint(jax.random.fold_in(key, 31), (1, 1, CHANNELS), 0, 2)
    channel_sign = (2 * sign_bits - 1).astype(jnp.float32)
    spread = jax.random.uniform(jax.random.fold_in(key, 32), (2, STATES, CHANNELS), jnp.float32, 0.5, 1.0)
    coherent = 4.0 * channel_sign * spread * (1.0 / math.sqrt(STATES * CHANNELS))
    noise = jnp.clip(jax.random.normal(jax.random.fold_in(key, 33), (2, STATES, CHANNELS), jnp.float32), -4.0, 4.0)
    return (coherent + noise * (1.0 / math.sqrt(STATES))).astype(jnp.float32)


def draw_inner_wave(key, part):
    noise = 1.5 * jnp.clip(jax.random.normal(jax.random.fold_in(key, 41), (2, STATES), jnp.float32), -4.0, 4.0)
    return (4.0 + noise).astype(jnp.float32)


def steps_of(rng, dims, shards, low, high):
    def one(axis_at, blocks):
        steps = jax.random.uniform(jax.random.fold_in(jax.random.fold_in(rng, 6), axis_at), (blocks,), jnp.float32, low / len(shards), high / len(shards))
        return jnp.repeat(jnp.exp(steps), dims[axis_at] // blocks).reshape((-1,) + (1,) * (len(dims) - axis_at - 1))

    level = one(*shards[0])
    for cut in shards[1:]:
        level = level * one(*cut)
    return level


def centred(key, extent, width, reach, pieces=(), held_as=jnp.bfloat16):
    array = width * jax.random.normal(key, extent, jnp.float32)
    if pieces:
        array = array * steps_of(key, extent, pieces, -0.22, 0.18)
    return jnp.clip(array, -reach, reach).astype(held_as)


def setup_inputs(seed: int = 0) -> dict:
    keys = jax.random.split(jax.random.key(seed), 10)
    outer_wave = centred(keys[0], (2, CHANNELS, RADIAL), 0.5, 3.0, ((1, 4), (2, 128)), jnp.float32)
    inner_wave = draw_inner_wave(jax.random.fold_in(keys[9], 71), 0)
    surface = draw_surface(jax.random.fold_in(keys[9], 71), 0)
    energies = jnp.clip(-2.0 + 102.0 * jax.random.uniform(keys[3], (STATES,), jnp.float32) ** steps_of(keys[3], (STATES,), ((0, 512),), -0.2, 0.2), -2.0, 100.0)
    coefficients = draw_coefficients(jax.random.fold_in(keys[9], 71), 0)
    block_cols = draw_block_cols(jax.random.fold_in(keys[9], 71), 0)
    block_kind = draw_block_kind(jax.random.fold_in(keys[9], 71), 0)
    polarisation = draw_polarisation(jax.random.fold_in(keys[9], 71), 0)
    laser_field = jnp.clip(jax.random.uniform(keys[8], (3,), jnp.float32, -0.05, 0.05), -0.05, 0.05)
    return dict(outer_wave=outer_wave, inner_wave=inner_wave, surface=surface, energies=energies, coefficients=coefficients, block_cols=block_cols, block_kind=block_kind, polarisation=polarisation, laser_field=laser_field)


inner_radius = 20.0
grid_step = 0.08
time_step = 0.01
stencil_scale = 1.0 / (24.0 * grid_step * grid_step)
taylor_terms = 10
squarings = 7
highest = lax.Precision.HIGHEST

def radial_factor(kind_map, polar_map, laser_field, radius):
    radius_ratio = inner_radius / radius
    dipole_like = radius_ratio * radius_ratio
    quadrupole_like = dipole_like * radius_ratio
    chosen = lax.optimization_barrier(jnp.sum(jnp.where(polar_map[..., None] == jnp.arange(3, dtype=jnp.int32), laser_field, 0.0), axis=-1))
    laser_term = chosen[..., None] * radius
    kind_wide = kind_map[..., None]
    return jnp.where(kind_wide == 0, dipole_like, jnp.where(kind_wide == 1, quadrupole_like, laser_term))

def kinetic(padded):
    return stencil_scale * (padded[:, :, :-4] - 16.0 * padded[:, :, 1:-3] + 30.0 * padded[:, :, 2:-2] - 16.0 * padded[:, :, 3:-1] + padded[:, :, 4:])

def complex_scale(scale_real, scale_imag, vector):
    return jnp.stack([scale_real * vector[0] - scale_imag * vector[1], scale_real * vector[1] + scale_imag * vector[0]])

def propagate(hess_real, hess_imag):
    top_half = jnp.concatenate([time_step * hess_imag, time_step * hess_real], axis=1)
    bottom_half = jnp.concatenate([-time_step * hess_real, time_step * hess_imag], axis=1)
    scaled_block = jnp.concatenate([top_half, bottom_half], axis=0) / 2.0 ** squarings
    identity = jnp.eye(2 * ITERS, dtype=jnp.float32)
    series = identity
    for degree in range(taylor_terms, 0, -1):
        series = identity + jnp.dot(scaled_block, series, precision=highest) / degree
    for repeat in range(squarings):
        series = jnp.dot(series, series, precision=highest)
    return (series[:ITERS, 0], series[ITERS:, 0])

def couple_all(outer, coefficients, block_cols, block_kind, polarisation, laser_field, radius):
    grouped = outer.reshape(2, BLOCKS, BS, RADIAL)

    def one_row(row_items):
        row_coef, row_cols, row_kind, row_polar = row_items
        picked = jnp.take(grouped, row_cols, axis=1)
        factor = radial_factor(row_kind, row_polar, laser_field, radius)
        product = jnp.einsum('sab,xsbr->xsar', row_coef, picked, precision=highest)
        return lax.optimization_barrier(jnp.sum(product * factor[None, :, None, :], axis=1))
    row_images = lax.map(one_row, (coefficients, block_cols, block_kind, polarisation))
    return jnp.transpose(row_images, (1, 0, 2, 3)).reshape(2, CHANNELS, RADIAL)

def apply_operator(outer, inner, surface, energies, coefficients, block_cols, block_kind, polarisation, laser_field, radius):
    ghosts = jnp.einsum('xk,lkc->xlc', inner, surface, precision=highest)
    lower_rim = jnp.stack([ghosts[:, 1], ghosts[:, 0]], axis=2)
    upper_rim = jnp.zeros_like(lower_rim)
    padded = jnp.concatenate([lower_rim, outer, upper_rim], axis=2)
    outer_image = kinetic(padded) + couple_all(outer, coefficients, block_cols, block_kind, polarisation, laser_field, radius)
    mixed_edge = -16.0 * outer[:, :, 0] + outer[:, :, 1]
    inner_image = energies * inner + stencil_scale * (jnp.einsum('xc,kc->xk', mixed_edge, surface[0], precision=highest) + jnp.einsum('xc,kc->xk', outer[:, :, 0], surface[1], precision=highest))
    return (outer_image, inner_image)

def reference(outer_wave, inner_wave, surface, energies, coefficients, block_cols, block_kind, polarisation, laser_field):
    radius = inner_radius + (jnp.arange(RADIAL, dtype=jnp.int32) + 1).astype(jnp.float32) * grid_step
    start_sq = jnp.sum(outer_wave * outer_wave) + jnp.sum(inner_wave * inner_wave)
    start_norm = jnp.sqrt(start_sq + 1e-06)
    basis_outer = [outer_wave / start_norm]
    basis_inner = [inner_wave / start_norm]
    hess_real = jnp.zeros((ITERS, ITERS), jnp.float32)
    hess_imag = jnp.zeros((ITERS, ITERS), jnp.float32)
    for column in range(ITERS):
        w_outer, w_inner = apply_operator(basis_outer[column], basis_inner[column], surface, energies, coefficients, block_cols, block_kind, polarisation, laser_field, radius)
        reals = []
        imags = []
        for vec_outer, vec_inner in zip(basis_outer, basis_inner):
            reals.append(jnp.sum(vec_outer * w_outer) + jnp.sum(vec_inner * w_inner))
            imags.append(jnp.sum(vec_outer[0] * w_outer[1] - vec_outer[1] * w_outer[0]) + jnp.sum(vec_inner[0] * w_inner[1] - vec_inner[1] * w_inner[0]))
        proj_real = jnp.stack(reals)
        proj_imag = jnp.stack(imags)
        for row_index in range(column + 1):
            w_outer = w_outer - complex_scale(proj_real[row_index], proj_imag[row_index], basis_outer[row_index])
            w_inner = w_inner - complex_scale(proj_real[row_index], proj_imag[row_index], basis_inner[row_index])
        hess_real = hess_real.at[:column + 1, column].set(proj_real)
        hess_imag = hess_imag.at[:column + 1, column].set(proj_imag)
        if column + 1 < ITERS:
            norm_sq = jnp.sum(w_outer * w_outer) + jnp.sum(w_inner * w_inner)
            next_norm = jnp.sqrt(norm_sq + 1e-06)
            hess_real = hess_real.at[column + 1, column].set(next_norm)
            basis_outer.append(w_outer / next_norm)
            basis_inner.append(w_inner / next_norm)
    coef_real, coef_imag = propagate(hess_real, hess_imag)
    accum_outer = jnp.zeros_like(outer_wave)
    accum_inner = jnp.zeros_like(inner_wave)
    for column in range(ITERS):
        accum_outer = accum_outer + complex_scale(coef_real[column], coef_imag[column], basis_outer[column])
        accum_inner = accum_inner + complex_scale(coef_real[column], coef_imag[column], basis_inner[column])
    return (accum_outer * start_norm, accum_inner * start_norm)
```

```python
import jax
import jax.numpy as jnp
import numpy as np
from jax import lax
from jax.sharding import PartitionSpec as P

ITERS = 4


inner_radius = 20.0
grid_step = 0.08
time_step = 0.01
stencil_scale = 1.0 / (24.0 * grid_step * grid_step)
taylor_terms = 10
squarings = 7
highest = lax.Precision.HIGHEST


def radial_factor(kind_map, polar_map, laser_field, radius):
    radius_ratio = inner_radius / radius
    dipole_like = radius_ratio * radius_ratio
    quadrupole_like = dipole_like * radius_ratio
    chosen = jnp.sum(
        jnp.where(polar_map[..., None] == jnp.arange(3, dtype=jnp.int32), laser_field, 0.0), axis=-1
    )
    laser_term = chosen[..., None] * radius
    kind_wide = kind_map[..., None]
    return jnp.where(
        kind_wide == 0, dipole_like, jnp.where(kind_wide == 1, quadrupole_like, laser_term)
    )


def halo(x, axis, width):
    size, length = lax.axis_size(axis), x.shape[2]
    up = [(i, i + 1) for i in range(size - 1)]
    down = [(j, i) for i, j in up]
    before = lax.ppermute(x[:, :, length - width :], axis, up)
    after = lax.ppermute(x[:, :, :width], axis, down)
    return jnp.concatenate([before, x, after], axis=2)


def kinetic(padded):
    return stencil_scale * (
        padded[:, :, :-4]
        - 16.0 * padded[:, :, 1:-3]
        + 30.0 * padded[:, :, 2:-2]
        - 16.0 * padded[:, :, 3:-1]
        + padded[:, :, 4:]
    )


def propagate(hess):
    scaled_block = jnp.zeros((2 * ITERS, 2 * ITERS), jnp.float32)
    for (i, j), (real, imag) in hess.items():
        for value, places in (
            (imag, ((i, j, 1.0), (i + ITERS, j + ITERS, 1.0))),
            (real, ((i, j + ITERS, 1.0), (i + ITERS, j, -1.0))),
        ):
            mask = np.zeros((2 * ITERS, 2 * ITERS), np.float32)
            for a, b, sign in places:
                mask[a, b] = sign
            scaled_block = scaled_block + (time_step * value) * mask
    scaled_block = scaled_block / 2.0**squarings
    identity = jnp.eye(2 * ITERS, dtype=jnp.float32)
    series = identity
    for degree in range(taylor_terms, 0, -1):
        series = identity + jnp.dot(scaled_block, series, precision=highest) / degree
    for repeat in range(squarings):
        series = jnp.dot(series, series, precision=highest)
    return (series[:ITERS, 0], series[ITERS:, 0])


def combine(scale, vector, terms):
    real, imag = (scale * vector[0], scale * vector[1])
    for (coef_real, coef_imag), other in terms:
        real = real - (coef_real * other[0] - coef_imag * other[1])
        imag = imag - (coef_real * other[1] + coef_imag * other[0])
    return jnp.stack([real, imag])


def per_device(
    outer_wave,
    inner_wave,
    surface,
    energies,
    coefficients,
    block_cols,
    block_kind,
    polarisation,
    laser_field,
):
    sec_index = lax.axis_index("sec")
    ch_index = lax.axis_index("ch")
    ch_count = lax.axis_size("ch")
    ch_dev = outer_wave.shape[1]
    rad_dev = outer_wave.shape[2]
    block_size = coefficients.shape[2]
    rows_dev = coefficients.shape[0]
    positions = sec_index * rad_dev + jnp.arange(rad_dev, dtype=jnp.int32)
    radius = inner_radius + (positions + 1).astype(jnp.float32) * grid_step
    first_sector = (sec_index == 0).astype(jnp.float32)
    local_cols = lax.dynamic_slice_in_dim(block_cols, ch_index * rows_dev, rows_dev, 0)
    local_kind = lax.dynamic_slice_in_dim(block_kind, ch_index * rows_dev, rows_dev, 0)
    local_polar = lax.dynamic_slice_in_dim(polarisation, ch_index * rows_dev, rows_dev, 0)
    local_factor = radial_factor(local_kind, local_polar, laser_field, radius)
    lane = lax.broadcasted_iota(jnp.int32, (1, 1, rad_dev), 2)

    def local_part(vector):
        outer, inner = vector
        full_rows = lax.all_gather(outer, "ch", axis=1, tiled=True)
        grouped = full_rows.reshape(2, -1, block_size, rad_dev)
        picked = jnp.take(grouped, local_cols, axis=1)
        product = jnp.einsum("lsab,xlsbr->xlsar", coefficients, picked, precision=highest)
        image = kinetic(halo(outer, "sec", 2)) + jnp.sum(
            product * local_factor[None, :, :, None, :], axis=2
        ).reshape(2, ch_dev, rad_dev)
        return (image, energies * inner)

    def with_boundary(image, ghosts, edges):
        outer, inner = image
        at_zero = (-16.0 * ghosts[:, 0] + ghosts[:, 1]) * (stencil_scale * first_sector)
        at_one = ghosts[:, 0] * (stencil_scale * first_sector)
        rim = jnp.where(
            lane == 0, at_zero[:, :, None], jnp.where(lane == 1, at_one[:, :, None], 0.0)
        )
        mixed = jnp.stack([-16.0 * edges[:, 0] + edges[:, 1], edges[:, 0]], axis=1)
        inner_add = jnp.einsum("xlc,lkc->xk", mixed, surface, precision=highest)
        return (outer + rim, inner + stencil_scale * inner_add)

    def reduce_all(vector, scalars):
        outer, inner = vector
        partial_sum = jnp.einsum("xk,lkc->xlc", inner, surface, precision=highest)
        edge_pair = jnp.stack([outer[:, :, 0], outer[:, :, 1]], axis=1) * first_sector
        edge_blank = jnp.zeros((2, 2, ch_dev * ch_count), jnp.float32)
        edge_full = lax.dynamic_update_slice_in_dim(edge_blank, edge_pair, ch_index * ch_dev, 2)
        sums, edges, totals = lax.psum(
            (partial_sum, edge_full, jnp.stack(scalars)), ("sec", "ch")
        )
        ghosts = lax.dynamic_slice_in_dim(sums, ch_index * ch_dev, ch_dev, 2)
        return (ghosts, edges, totals)

    def norm_of(vector):
        return jnp.sum(vector[0] * vector[0]) + jnp.sum(vector[1] * vector[1])

    def product_of(a, b):
        real = jnp.sum(a[0] * b[0]) + jnp.sum(a[1] * b[1])
        imag = jnp.sum(a[0][0] * b[0][1] - a[0][1] * b[0][0]) + jnp.sum(
            a[1][0] * b[1][1] - a[1][1] * b[1][0]
        )
        return [real, imag]

    current = (outer_wave, inner_wave)
    image = local_part(current)
    ghosts, edges, totals = reduce_all(current, [norm_of(current)])
    norms = [jnp.sqrt(totals[0] + 1e-06)]
    basis, images, rims = [current], [image], [(ghosts, edges)]
    hess = {}
    for column in range(ITERS):
        applied = with_boundary(images[column], *rims[column])
        scalars = []
        for vector in basis:
            scalars += product_of(vector, applied)
        scalars.append(norm_of(basis[column]))
        if column + 1 < ITERS:
            applied_image = local_part(applied)
            ghosts, edges, totals = reduce_all(applied, scalars)
        else:
            totals = lax.psum(jnp.stack(scalars), ("sec", "ch"))
        if column:
            norms.append(jnp.sqrt(totals[2 * column + 2] + 1e-06))
            hess[column, column - 1] = (norms[column], jnp.zeros((), jnp.float32))
        terms = []
        for row in range(column + 1):
            scale = 1.0 / (norms[row] * norms[column])
            real, imag = (totals[2 * row] * scale, totals[2 * row + 1] * scale)
            hess[row, column] = (real, imag)
            terms.append((real / norms[row], imag / norms[row]))
        if column + 1 < ITERS:
            inverse = 1.0 / norms[column]

            def advance(new, olds):
                return combine(inverse, new, list(zip(terms, olds)))

            basis.append(
                tuple(advance(applied[k], [old[k] for old in basis]) for k in range(2))
            )
            images.append(
                tuple(advance(applied_image[k], [old[k] for old in images]) for k in range(2))
            )
            new_rim = (ghosts, edges)
            rims.append(tuple(advance(new_rim[k], [old[k] for old in rims]) for k in range(2)))
    coef_real, coef_imag = propagate(hess)
    outputs = []
    for k in range(2):
        terms = []
        for column in range(ITERS):
            scale = norms[0] / norms[column]
            terms.append(((-coef_real[column] * scale, -coef_imag[column] * scale), basis[column][k]))
        outputs.append(combine(0.0, basis[0][k], terms))
    return tuple(outputs)


def solution(mesh):
    placed = (
        P(None, "ch", "sec"),
        P(None, ("sec", "ch")),
        P(None, ("sec", "ch"), None),
        P(("sec", "ch")),
        P("ch", None, None, None),
        P(),
        P(),
        P(),
        P(),
    )
    return jax.shard_map(
        per_device,
        mesh=mesh,
        in_specs=placed,
        out_specs=(P(None, "ch", "sec"), P(None, ("sec", "ch"))),
        check_vma=False,
    )
```

```python
import functools

import jax
import jax.numpy as jnp
import numpy as np
from jax import lax
from jax.experimental import pallas as pl
from jax.experimental.pallas import tpu as pltpu
from jax.sharding import PartitionSpec as P

ITERS = 4


inner_radius = 20.0
grid_step = 0.08
time_step = 0.01
stencil_scale = 1.0 / (24.0 * grid_step * grid_step)
taylor_terms = 10
squarings = 7
highest = lax.Precision.HIGHEST


def radial_factor(kind_map, polar_map, laser_field, radius):
    radius_ratio = inner_radius / radius
    dipole_like = radius_ratio * radius_ratio
    quadrupole_like = dipole_like * radius_ratio
    chosen = jnp.sum(
        jnp.where(polar_map[..., None] == jnp.arange(3, dtype=jnp.int32), laser_field, 0.0), axis=-1
    )
    laser_term = chosen[..., None] * radius
    kind_wide = kind_map[..., None]
    return jnp.where(
        kind_wide == 0, dipole_like, jnp.where(kind_wide == 1, quadrupole_like, laser_term)
    )


MESH = pl.DeviceIdType.MESH


def exchange_kernel(dims, bulk, *refs):
    y_size, z_size, c_size, x_size = dims
    if bulk:
        (ghost_in, edge_in, first_in, last_in, outer_in) = refs[:5]
        (sum_out, edge_out, before_out, after_out, full_out) = refs[5:10]
        refs = refs[10:]
    else:
        (ghost_in, sum_out) = refs[:2]
        refs = refs[2:]
    (x_slots, c_slots, z_slots, y_slots) = refs[:4]
    (x_send, x_recv, c_send, c_recv, z_send, z_recv, y_send, y_recv) = refs[4:12]
    if bulk:
        (bulk_send, bulk_recv, side_send, side_recv, edge_send, edge_recv, own_sem) = refs[12:]
    sec = lax.axis_index("sec")
    x = lax.axis_index("ch")
    c = lax.rem(sec, c_size)
    z = lax.rem(sec // c_size, z_size)
    y = sec // (c_size * z_size)
    sec_size = y_size * z_size * c_size
    rows = ghost_in.shape[1]

    def x_peer(d):
        return {"ch": lax.rem(x + d, x_size)}

    def c_peer(d):
        return {"sec": (y * z_size + z) * c_size + lax.rem(c + d, c_size)}

    def z_peer(d):
        return {"sec": (y * z_size + lax.rem(z + d, z_size)) * c_size + c}

    def y_peer(d):
        return {"sec": (lax.rem(y + d, y_size) * z_size + z) * c_size + c}

    up = {"sec": lax.rem(sec + 1, sec_size)}
    down = {"sec": lax.rem(sec + sec_size - 1, sec_size)}

    greeted = []
    for size, peer in ((x_size, x_peer), (c_size, c_peer), (z_size, z_peer), (y_size, y_peer)):
        greeted += [peer(d) for d in range(1, size)]
    if bulk:
        greeted += [up, down]
    barrier = pltpu.get_barrier_semaphore()
    for peer in greeted:
        pl.semaphore_signal(barrier, inc=1, device_id=peer, device_id_type=MESH)
    pl.semaphore_wait(barrier, len(greeted))

    def remote(src, dst, send, recv, peer):
        copy = pltpu.make_async_remote_copy(
            src_ref=src,
            dst_ref=dst,
            send_sem=send,
            recv_sem=recv,
            device_id=peer,
            device_id_type=MESH,
        )
        copy.start()
        return copy

    x_copies = []
    for d in range(1, x_size):
        x_copies.append(
            remote(
                ghost_in.at[lax.rem(x + d, x_size)],
                x_slots.at[x],
                x_send.at[d - 1],
                x_recv.at[d - 1],
                x_peer(d),
            )
        )
    later = []
    if bulk:
        later.append(remote(last_in, before_out, side_send.at[0], side_recv.at[0], up))
        later.append(remote(first_in, after_out, side_send.at[1], side_recv.at[1], down))
        for d in range(1, x_size):
            later.append(
                remote(
                    outer_in, full_out.at[x], bulk_send.at[d - 1], bulk_recv.at[d - 1], x_peer(d)
                )
            )
        own = pltpu.make_async_copy(outer_in, full_out.at[x], own_sem)
        own.start()
        later.append(own)
    x_slots[x] = ghost_in[x]
    for copy in x_copies:
        copy.wait()

    def total(slots, size):
        value = slots[0]
        for k in range(1, size):
            value = value + slots[k]
        return value

    c_slots[c, 0:rows] = total(x_slots, x_size)
    if bulk:
        c_slots[c, rows:] = edge_in[...]

    def stage(slots, me, size, peer, send, recv):
        copies = []
        for d in range(1, size):
            copies.append(
                remote(slots.at[me], slots.at[me], send.at[d - 1], recv.at[d - 1], peer(d))
            )
        for copy in copies:
            copy.wait()
        return total(slots, size)

    z_slots[z] = stage(c_slots, c, c_size, c_peer, c_send, c_recv)
    y_slots[y] = stage(z_slots, z, z_size, z_peer, z_send, z_recv)
    value = stage(y_slots, y, y_size, y_peer, y_send, y_recv)
    sum_out[...] = value[0:rows]
    if bulk:
        edge_out[x] = value[rows:]
        copies = []
        for d in range(1, x_size):
            copies.append(
                remote(
                    edge_out.at[x],
                    edge_out.at[x],
                    edge_send.at[d - 1],
                    edge_recv.at[d - 1],
                    x_peer(d),
                )
            )
        for copy in copies + later:
            copy.wait()


def exchange(dims, ghosts, edges=None, first=None, last=None, outer=None):
    bulk = outer is not None
    y_size, z_size, c_size, x_size = dims
    x_count, rows, lanes = ghosts.shape
    vmem = pl.BlockSpec(memory_space=pltpu.VMEM)
    hbm = pl.BlockSpec(memory_space=pl.ANY)
    shape = functools.partial(jax.ShapeDtypeStruct, dtype=jnp.float32)
    outs = [shape((rows, lanes))]
    args = [ghosts]
    width = rows
    if bulk:
        args += [edges, first, last, outer]
        side = edges.shape
        width = rows + side[0]
        outs += [shape((x_size,) + side), shape(side), shape(side), shape((x_size,) + outer.shape)]
    dma = pltpu.SemaphoreType.DMA
    scratch = [
        pltpu.VMEM((x_size, rows, lanes), jnp.float32),
        pltpu.VMEM((c_size, width, lanes), jnp.float32),
        pltpu.VMEM((z_size, width, lanes), jnp.float32),
        pltpu.VMEM((y_size, width, lanes), jnp.float32),
    ]
    for size in (x_size, c_size, z_size, y_size):
        scratch += [dma((size - 1,)), dma((size - 1,))]
    if bulk:
        scratch += [dma((x_size - 1,)), dma((x_size - 1,)), dma((2,)), dma((2,))]
        scratch += [dma((x_size - 1,)), dma((x_size - 1,)), dma]
    return pl.pallas_call(
        functools.partial(exchange_kernel, dims, bulk),
        out_shape=outs,
        in_specs=[vmem] * len(args),
        out_specs=[vmem] * 4 + [hbm] if bulk else [vmem],
        scratch_shapes=scratch,
        compiler_params=pltpu.CompilerParams(collective_id=1 if bulk else 2, has_side_effects=True),
        name="exchange_bulk" if bulk else "exchange_sums",
    )(*args)


def kinetic(padded):
    return stencil_scale * (
        padded[:, :, :-4]
        - 16.0 * padded[:, :, 1:-3]
        + 30.0 * padded[:, :, 2:-2]
        - 16.0 * padded[:, :, 3:-1]
        + padded[:, :, 4:]
    )


def propagate(hess):
    scaled_block = jnp.zeros((2 * ITERS, 2 * ITERS), jnp.float32)
    for (i, j), (real, imag) in hess.items():
        for value, places in (
            (imag, ((i, j, 1.0), (i + ITERS, j + ITERS, 1.0))),
            (real, ((i, j + ITERS, 1.0), (i + ITERS, j, -1.0))),
        ):
            mask = np.zeros((2 * ITERS, 2 * ITERS), np.float32)
            for a, b, sign in places:
                mask[a, b] = sign
            scaled_block = scaled_block + (time_step * value) * mask
    scaled_block = scaled_block / 2.0**squarings
    identity = jnp.eye(2 * ITERS, dtype=jnp.float32)
    series = identity
    for degree in range(taylor_terms, 0, -1):
        series = identity + jnp.dot(scaled_block, series, precision=highest) / degree
    for repeat in range(squarings):
        series = jnp.dot(series, series, precision=highest)
    return (series[:ITERS, 0], series[ITERS:, 0])


def combine(scale, vector, terms):
    real, imag = (scale * vector[0], scale * vector[1])
    for (coef_real, coef_imag), other in terms:
        real = real - (coef_real * other[0] - coef_imag * other[1])
        imag = imag - (coef_real * other[1] + coef_imag * other[0])
    return jnp.stack([real, imag])


def per_device(
    dims,
    outer_wave,
    inner_wave,
    surface,
    energies,
    coefficients,
    block_cols,
    block_kind,
    polarisation,
    laser_field,
):
    sec_index = lax.axis_index("sec")
    ch_index = lax.axis_index("ch")
    ch_count = lax.axis_size("ch")
    ch_dev = outer_wave.shape[1]
    rad_dev = outer_wave.shape[2]
    block_size = coefficients.shape[2]
    rows_dev = coefficients.shape[0]
    positions = sec_index * rad_dev + jnp.arange(rad_dev, dtype=jnp.int32)
    radius = inner_radius + (positions + 1).astype(jnp.float32) * grid_step
    first_sector = (sec_index == 0).astype(jnp.float32)
    last_sector = (sec_index == lax.axis_size("sec") - 1).astype(jnp.float32)
    pair_rows = 4 * ch_dev // 128
    side_rows = (pair_rows // 8 + 1) * 8
    local_cols = lax.dynamic_slice_in_dim(block_cols, ch_index * rows_dev, rows_dev, 0)
    local_kind = lax.dynamic_slice_in_dim(block_kind, ch_index * rows_dev, rows_dev, 0)
    local_polar = lax.dynamic_slice_in_dim(polarisation, ch_index * rows_dev, rows_dev, 0)
    local_factor = radial_factor(local_kind, local_polar, laser_field, radius)
    lane = lax.broadcasted_iota(jnp.int32, (1, 1, rad_dev), 2)

    def padded_rows(value, count):
        return jnp.concatenate([value, jnp.zeros((count - value.shape[0], 128), jnp.float32)], axis=0)

    def column_rows(outer, start):
        pair = jnp.stack([outer[:, :, start], outer[:, :, start + 1]], axis=1)
        return padded_rows(pair.reshape(pair_rows, 128), side_rows)

    def side_columns(rows, keep):
        pair = rows[:pair_rows].reshape(2, 2, ch_dev) * keep
        return jnp.transpose(pair, (0, 2, 1))

    def scalar_row(scalars):
        place = lax.broadcasted_iota(jnp.int32, (1, 128), 1)
        row = jnp.zeros((1, 128), jnp.float32)
        for k, value in enumerate(scalars):
            row = jnp.where(place == k, value, row)
        return row

    def exchanged(vector, scalars):
        outer, inner = vector
        partial_sum = jnp.einsum("xk,lkc->xlc", inner, surface, precision=highest)
        sliced = jnp.transpose(partial_sum.reshape(2, 2, ch_count, ch_dev), (2, 0, 1, 3))
        sliced = sliced.reshape(ch_count, pair_rows, 128)
        tail = padded_rows(scalar_row(scalars), side_rows - pair_rows)
        tail = jnp.broadcast_to(tail[None], (ch_count,) + tail.shape)
        first = column_rows(outer, 0)
        last = column_rows(outer, rad_dev - 2)
        sums, edge_rows, before, after, full = exchange(
            dims, jnp.concatenate([sliced, tail], axis=1), first * first_sector, first, last, outer
        )
        ghosts = sums[:pair_rows].reshape(2, 2, ch_dev)
        edges = edge_rows[:, :pair_rows].reshape(ch_count, 2, 2, ch_dev)
        edges = jnp.transpose(edges, (1, 2, 0, 3)).reshape(2, 2, ch_count * ch_dev)
        grouped = full.reshape(ch_count, 2, rows_dev, block_size, rad_dev)
        picked = grouped[local_cols // rows_dev, :, local_cols % rows_dev]
        product = jnp.einsum("lsab,lsxbr->xlsar", coefficients, picked, precision=highest)
        padded = jnp.concatenate(
            [side_columns(before, 1.0 - first_sector), outer, side_columns(after, 1.0 - last_sector)],
            axis=2,
        )
        image = kinetic(padded) + jnp.sum(
            product * local_factor[None, :, :, None, :], axis=2
        ).reshape(2, ch_dev, rad_dev)
        return (ghosts, edges, sums[pair_rows], (image, energies * inner))

    def with_boundary(image, ghosts, edges):
        outer, inner = image
        at_zero = (-16.0 * ghosts[:, 0] + ghosts[:, 1]) * (stencil_scale * first_sector)
        at_one = ghosts[:, 0] * (stencil_scale * first_sector)
        rim = jnp.where(
            lane == 0, at_zero[:, :, None], jnp.where(lane == 1, at_one[:, :, None], 0.0)
        )
        mixed = jnp.stack([-16.0 * edges[:, 0] + edges[:, 1], edges[:, 0]], axis=1)
        inner_add = jnp.einsum("xlc,lkc->xk", mixed, surface, precision=highest)
        return (outer + rim, inner + stencil_scale * inner_add)

    def norm_of(vector):
        return jnp.sum(vector[0] * vector[0]) + jnp.sum(vector[1] * vector[1])

    def product_of(a, b):
        real = jnp.sum(a[0] * b[0]) + jnp.sum(a[1] * b[1])
        imag = jnp.sum(a[0][0] * b[0][1] - a[0][1] * b[0][0]) + jnp.sum(
            a[1][0] * b[1][1] - a[1][1] * b[1][0]
        )
        return [real, imag]

    current = (outer_wave, inner_wave)
    ghosts, edges, totals, image = exchanged(current, [norm_of(current)])
    norms = [jnp.sqrt(totals[0] + 1e-06)]
    basis, images, rims = [current], [image], [(ghosts, edges)]
    hess = {}
    for column in range(ITERS):
        applied = with_boundary(images[column], *rims[column])
        scalars = []
        for vector in basis:
            scalars += product_of(vector, applied)
        scalars.append(norm_of(basis[column]))
        if column + 1 < ITERS:
            ghosts, edges, totals, applied_image = exchanged(applied, scalars)
        else:
            row = padded_rows(scalar_row(scalars), 8)
            totals = exchange(dims, jnp.broadcast_to(row[None], (ch_count, 8, 128)))[0][0]
        if column:
            norms.append(jnp.sqrt(totals[2 * column + 2] + 1e-06))
            hess[column, column - 1] = (norms[column], jnp.zeros((), jnp.float32))
        terms = []
        for row in range(column + 1):
            scale = 1.0 / (norms[row] * norms[column])
            real, imag = (totals[2 * row] * scale, totals[2 * row + 1] * scale)
            hess[row, column] = (real, imag)
            terms.append((real / norms[row], imag / norms[row]))
        if column + 1 < ITERS:
            inverse = 1.0 / norms[column]

            def advance(new, olds):
                return combine(inverse, new, list(zip(terms, olds)))

            basis.append(
                tuple(advance(applied[k], [old[k] for old in basis]) for k in range(2))
            )
            images.append(
                tuple(advance(applied_image[k], [old[k] for old in images]) for k in range(2))
            )
            new_rim = (ghosts, edges)
            rims.append(tuple(advance(new_rim[k], [old[k] for old in rims]) for k in range(2)))
    coef_real, coef_imag = propagate(hess)
    outputs = []
    for k in range(2):
        terms = []
        for column in range(ITERS):
            scale = norms[0] / norms[column]
            terms.append(((-coef_real[column] * scale, -coef_imag[column] * scale), basis[column][k]))
        outputs.append(combine(0.0, basis[0][k], terms))
    return tuple(outputs)


def solution(mesh):
    placed = (
        P(None, "ch", "sec"),
        P(None, ("sec", "ch")),
        P(None, ("sec", "ch"), None),
        P(("sec", "ch")),
        P("ch", None, None, None),
        P(),
        P(),
        P(),
        P(),
    )
    return jax.shard_map(
        functools.partial(per_device, (8, 8, 2, 4)),
        mesh=mesh,
        in_specs=placed,
        out_specs=(P(None, "ch", "sec"), P(None, ("sec", "ch"))),
        check_vma=False,
    )
```

```python
import functools

import jax
import jax.numpy as jnp
import numpy as np
from jax import lax
from jax.experimental import pallas as pl
from jax.experimental.pallas import tpu as pltpu
from jax.sharding import PartitionSpec as P

ITERS = 4


inner_radius = 20.0
grid_step = 0.08
time_step = 0.01
stencil_scale = 1.0 / (24.0 * grid_step * grid_step)
taylor_terms = 10
squarings = 7
highest = lax.Precision.HIGHEST


def radial_factor(kind_map, polar_map, laser_field, radius):
    radius_ratio = inner_radius / radius
    dipole_like = radius_ratio * radius_ratio
    quadrupole_like = dipole_like * radius_ratio
    chosen = jnp.sum(
        jnp.where(polar_map[..., None] == jnp.arange(3, dtype=jnp.int32), laser_field, 0.0), axis=-1
    )
    laser_term = chosen[..., None] * radius
    kind_wide = kind_map[..., None]
    return jnp.where(
        kind_wide == 0, dipole_like, jnp.where(kind_wide == 1, quadrupole_like, laser_term)
    )


MESH = pl.DeviceIdType.MESH


def exchange_kernel(dims, bulk, *refs):
    y_size, z_size, c_size, x_size = dims
    if bulk:
        (ghost_in, edge_in, first_in, last_in, outer_in) = refs[:5]
        (sum_out, edge_out, before_out, after_out, full_out) = refs[5:10]
        refs = refs[10:]
    else:
        (ghost_in, sum_out) = refs[:2]
        refs = refs[2:]
    (x_slots, c_slots, z_slots, y_slots) = refs[:4]
    (x_send, x_recv, c_send, c_recv, z_send, z_recv, y_send, y_recv) = refs[4:12]
    if bulk:
        (bulk_send, bulk_recv, side_send, side_recv, edge_send, edge_recv, own_sem) = refs[12:]
    sec = lax.axis_index("sec")
    x = lax.axis_index("ch")
    c = lax.rem(sec, c_size)
    z = lax.rem(sec // c_size, z_size)
    y = sec // (c_size * z_size)
    sec_size = y_size * z_size * c_size
    rows = ghost_in.shape[1]

    def x_peer(d):
        return {"ch": lax.rem(x + d, x_size)}

    def c_peer(d):
        return {"sec": (y * z_size + z) * c_size + lax.rem(c + d, c_size)}

    def z_peer(d):
        return {"sec": (y * z_size + lax.rem(z + d, z_size)) * c_size + c}

    def y_peer(d):
        return {"sec": (lax.rem(y + d, y_size) * z_size + z) * c_size + c}

    up = {"sec": lax.rem(sec + 1, sec_size)}
    down = {"sec": lax.rem(sec + sec_size - 1, sec_size)}

    greeted = []
    for size, peer in ((x_size, x_peer), (c_size, c_peer), (z_size, z_peer), (y_size, y_peer)):
        greeted += [peer(d) for d in range(1, size)]
    if bulk:
        greeted += [up, down]
    barrier = pltpu.get_barrier_semaphore()
    for peer in greeted:
        pl.semaphore_signal(barrier, inc=1, device_id=peer, device_id_type=MESH)
    pl.semaphore_wait(barrier, len(greeted))

    def remote(src, dst, send, recv, peer):
        copy = pltpu.make_async_remote_copy(
            src_ref=src,
            dst_ref=dst,
            send_sem=send,
            recv_sem=recv,
            device_id=peer,
            device_id_type=MESH,
        )
        copy.start()
        return copy

    x_copies = []
    for d in range(1, x_size):
        x_copies.append(
            remote(
                ghost_in.at[lax.rem(x + d, x_size)],
                x_slots.at[x],
                x_send.at[d - 1],
                x_recv.at[d - 1],
                x_peer(d),
            )
        )
    later = []
    if bulk:
        later.append(remote(last_in, before_out, side_send.at[0], side_recv.at[0], up))
        later.append(remote(first_in, after_out, side_send.at[1], side_recv.at[1], down))
        for d in range(1, x_size):
            later.append(
                remote(
                    outer_in, full_out.at[x], bulk_send.at[d - 1], bulk_recv.at[d - 1], x_peer(d)
                )
            )
        own = pltpu.make_async_copy(outer_in, full_out.at[x], own_sem)
        own.start()
        later.append(own)
    x_slots[x] = ghost_in[x]
    for copy in x_copies:
        copy.wait()

    def total(slots, size):
        value = slots[0]
        for k in range(1, size):
            value = value + slots[k]
        return value

    c_slots[c, 0:rows] = total(x_slots, x_size)
    if bulk:
        c_slots[c, rows:] = edge_in[...]

    def stage(slots, me, size, peer, send, recv):
        copies = []
        for d in range(1, size):
            copies.append(
                remote(slots.at[me], slots.at[me], send.at[d - 1], recv.at[d - 1], peer(d))
            )
        for copy in copies:
            copy.wait()
        return total(slots, size)

    z_slots[z] = stage(c_slots, c, c_size, c_peer, c_send, c_recv)
    y_slots[y] = stage(z_slots, z, z_size, z_peer, z_send, z_recv)
    value = stage(y_slots, y, y_size, y_peer, y_send, y_recv)
    sum_out[...] = value[0:rows]
    if bulk:
        edge_out[x] = value[rows:]
        copies = []
        for d in range(1, x_size):
            copies.append(
                remote(
                    edge_out.at[x],
                    edge_out.at[x],
                    edge_send.at[d - 1],
                    edge_recv.at[d - 1],
                    x_peer(d),
                )
            )
        for copy in copies + later:
            copy.wait()


def exchange(dims, ghosts, edges=None, first=None, last=None, outer=None):
    bulk = outer is not None
    y_size, z_size, c_size, x_size = dims
    x_count, rows, lanes = ghosts.shape
    vmem = pl.BlockSpec(memory_space=pltpu.VMEM)
    hbm = pl.BlockSpec(memory_space=pl.ANY)
    shape = functools.partial(jax.ShapeDtypeStruct, dtype=jnp.float32)
    outs = [shape((rows, lanes))]
    args = [ghosts]
    width = rows
    if bulk:
        args += [edges, first, last, outer]
        side = edges.shape
        width = rows + side[0]
        outs += [shape((x_size,) + side), shape(side), shape(side), shape((x_size,) + outer.shape)]
    dma = pltpu.SemaphoreType.DMA
    scratch = [
        pltpu.VMEM((x_size, rows, lanes), jnp.float32),
        pltpu.VMEM((c_size, width, lanes), jnp.float32),
        pltpu.VMEM((z_size, width, lanes), jnp.float32),
        pltpu.VMEM((y_size, width, lanes), jnp.float32),
    ]
    for size in (x_size, c_size, z_size, y_size):
        scratch += [dma((size - 1,)), dma((size - 1,))]
    if bulk:
        scratch += [dma((x_size - 1,)), dma((x_size - 1,)), dma((2,)), dma((2,))]
        scratch += [dma((x_size - 1,)), dma((x_size - 1,)), dma]
    return pl.pallas_call(
        functools.partial(exchange_kernel, dims, bulk),
        out_shape=outs,
        in_specs=[vmem] * len(args),
        out_specs=[vmem] * 4 + [hbm] if bulk else [vmem],
        scratch_shapes=scratch,
        compiler_params=pltpu.CompilerParams(collective_id=1 if bulk else 2, has_side_effects=True),
        name="exchange_bulk" if bulk else "exchange_sums",
    )(*args)


def exact_dot(a, b, dims=((1,), (0,))):
    return lax.dot_general(
        a, b, (dims, ((), ())), precision=highest, preferred_element_type=jnp.float32
    )


def full_sum(value):
    return jnp.sum(jnp.sum(value, axis=0, keepdims=True), axis=1, keepdims=True)


def tile_sum(value):
    return jnp.sum(value.reshape(value.shape[0] // 8, 8, value.shape[1]), axis=0)


def combine(scale, real, imag, terms):
    real, imag = (scale * real, scale * imag)
    for coef_real, coef_imag, other_real, other_imag in terms:
        real = real - (coef_real * other_real - coef_imag * other_imag)
        imag = imag - (coef_real * other_imag + coef_imag * other_real)
    return (real, imag)


def pick(row, k):
    lane = lax.broadcasted_iota(jnp.int32, row.shape, 1)
    return jnp.sum(jnp.where(lane == k, row, 0.0), axis=1, keepdims=True)


def pack(outer, inner, surface, flags, scalars, ghost_out, first_out, last_out, edge_out):
    ch_count = ghost_out.shape[0]
    bs = outer.shape[2]
    blocks = outer.shape[1] // bs
    ghost_out[...] = jnp.zeros_like(ghost_out)
    first_out[...] = jnp.zeros_like(first_out)
    last_out[...] = jnp.zeros_like(last_out)
    row_at = lax.broadcasted_iota(jnp.int32, (8, bs), 0)
    lane_at = lax.broadcasted_iota(jnp.int32, (8, bs), 1)
    wanted = jnp.where(row_at < 2, row_at, jnp.where(row_at < 4, row_at + bs - 4, -1))
    select = (lane_at == wanted).astype(jnp.float32)
    for x in range(2):
        for b in range(blocks):
            rows = exact_dot(select, outer[x, b * bs : (b + 1) * bs, :], ((1,), (1,)))
            for pt in range(2):
                at = pt * blocks + b
                first_out[x, at : at + 1, :] = rows[pt : pt + 1]
                last_out[x, at : at + 1, :] = rows[pt + 2 : pt + 3]
    edge_out[...] = first_out[...] * flags[0]
    for layer in range(2):
        sums = exact_dot(inner, surface[layer])
        for x in range(2):
            for p in range(ch_count):
                for b in range(blocks):
                    at, start = (layer * blocks + b, (p * blocks + b) * bs)
                    ghost_out[p, x, at : at + 1, :] = sums[x : x + 1, start : start + bs]
    put_scalars(scalars, ghost_out, 2 * blocks)


def put_scalars(scalars, ghost_out, at):
    lane = lax.broadcasted_iota(jnp.int32, (1, 128), 1)
    row = jnp.zeros((1, 128), jnp.float32)
    for k, value in enumerate(scalars):
        row = jnp.where(lane == k, value, row)
    for p in range(ghost_out.shape[0]):
        ghost_out[p, 0, at : at + 1, :] = row


def prepare_kernel(flags, outer, inner, surface, ghost_out, first_out, last_out, edge_out):
    value = full_sum(inner[...] * inner[...])
    for x in range(2):
        part = outer[x]
        value = value + full_sum(tile_sum(part * part))
    pack(outer, inner[...], surface, flags, [value], ghost_out, first_out, last_out, edge_out)


def step_kernel(column, last_step, *refs):
    refs = list(refs)
    take = lambda count: [refs.pop(0) for _ in range(count)]
    cols, flags, factor, coef, surface, energies = take(6)
    outer, inner, sums, edges, before, after, full = take(7)
    olds_sums = take(column)
    old_outer, old_inner = (take(column), take(column))
    old_image, old_image_inner = (take(column), take(column))
    old_ghost, old_edge = (take(column), take(column))
    if column:
        new_outer, new_inner, new_ghost, new_edge = take(4)
    else:
        new_outer, new_inner, new_ghost, new_edge = (outer, inner, sums, edges)
    image, image_inner, applied, applied_inner = take(4)
    if last_step:
        (ghost_out,) = take(1)
    else:
        ghost_out, first_out, last_out, edge_out = take(4)
    mixed = take(1)[0]
    bs = outer.shape[2]
    blocks = outer.shape[1] // bs
    slots = coef.shape[1]
    ch_count = edges.shape[0]
    at_row = 2 * blocks

    terms = []
    inverse = None
    if column:
        history = [ref[0, at_row : at_row + 1, :] for ref in olds_sums]
        history.append(sums[0, at_row : at_row + 1, :])
        roots = [lax.rsqrt(pick(history[0], 0) + 1e-06)]
        for k in range(1, column):
            roots.append(lax.rsqrt(pick(history[k + 1], 2 * k + 2) + 1e-06))
        inverse = roots[column - 1]
        for row in range(column):
            scale = roots[row] * roots[row] * inverse
            terms.append(
                (pick(history[column], 2 * row) * scale, pick(history[column], 2 * row + 1) * scale)
            )

    def advance(real, imag, others):
        return combine(
            inverse, real, imag, [t + o for t, o in zip(terms, others)]
        )

    if column:
        real, imag = advance(sums[0], sums[1], [(o[0], o[1]) for o in old_ghost])
        new_ghost[0] = real
        new_ghost[1] = imag
        for p in range(ch_count):
            real, imag = advance(edges[p, 0], edges[p, 1], [(o[p, 0], o[p, 1]) for o in old_edge])
            new_edge[p, 0] = real
            new_edge[p, 1] = imag
        real, imag = advance(
            inner[0:1], inner[1:2], [(o[0:1], o[1:2]) for o in old_inner]
        )
        new_inner[0:1] = real
        new_inner[1:2] = imag
        real, imag = advance(
            energies[...] * inner[0:1],
            energies[...] * inner[1:2],
            [(o[0:1], o[1:2]) for o in old_image_inner],
        )
        image_inner[0:1] = real
        image_inner[1:2] = imag
    else:
        image_inner[...] = energies[...] * inner[...]

    mixed[...] = jnp.zeros_like(mixed)
    for p in range(ch_count):
        for x in range(2):
            for b in range(blocks):
                start = (p * blocks + b) * bs
                zero = new_edge[p, x, b : b + 1, :]
                one = new_edge[p, x, blocks + b : blocks + b + 1, :]
                mixed[0, x : x + 1, start : start + bs] = -16.0 * zero + one
                mixed[1, x : x + 1, start : start + bs] = zero
    added = exact_dot(mixed[0], surface[0], ((1,), (1,)))
    added = added + exact_dot(mixed[1], surface[1], ((1,), (1,)))
    applied_inner[...] = image_inner[...] + stencil_scale * added[0:2]

    row_at = lax.broadcasted_iota(jnp.int32, (8, bs), 0)
    lane_at = lax.broadcasted_iota(jnp.int32, (8, bs), 1)

    def weight(row, lane, value):
        return jnp.where((row_at == row) & (lane_at == lane), value * stencil_scale, 0.0)

    weights = (
        weight(0, 0, 1.0)
        + weight(1, 0, -16.0)
        + weight(1, 1, 1.0)
        + weight(2, bs - 1, -16.0)
        + weight(2, bs - 2, 1.0)
        + weight(3, bs - 1, 1.0)
    )
    zeros = jnp.zeros((4, bs), jnp.float32)
    lane = lax.broadcasted_iota(jnp.int32, (bs, bs), 1)

    def rim(far, near, next0, next1):
        rows = jnp.concatenate([far, near, next0, next1, zeros], axis=0)
        return exact_dot(rows, weights, ((0,), (0,)))

    count = column + 1
    reals = [jnp.zeros((8, bs), jnp.float32) for _ in range(count)]
    imags = [jnp.zeros((8, bs), jnp.float32) for _ in range(count)]
    square = jnp.zeros((8, bs), jnp.float32)
    for b in range(blocks):
        rows = slice(b * bs, (b + 1) * bs)
        product = jnp.zeros((bs, 2 * bs), jnp.float32)
        for s in range(0, slots, 2):
            sides = []
            for t in (s, s + 1):
                col = cols[b, t]
                place = pl.ds(pl.multiple_of(lax.rem(col, blocks) * bs, bs), bs)
                owner = lax.div(col, blocks)
                scale = factor[b, t : t + 1, :]
                sides.append(
                    jnp.concatenate(
                        [full[owner, 0, place, :] * scale, full[owner, 1, place, :] * scale], axis=1
                    )
                )
            left = jnp.concatenate([coef[b, s], coef[b, s + 1]], axis=1)
            product = product + exact_dot(left, jnp.concatenate(sides, axis=0))
        parts = []
        for x in range(2):
            value = outer[x, rows, :]
            m1 = jnp.where(lane >= 1, pltpu.roll(value, 1, 1), 0.0)
            m2 = jnp.where(lane >= 2, pltpu.roll(value, 2, 1), 0.0)
            p1 = jnp.where(lane < bs - 1, pltpu.roll(value, bs - 1, 1), 0.0)
            p2 = jnp.where(lane < bs - 2, pltpu.roll(value, bs - 2, 1), 0.0)
            stencil = stencil_scale * (m2 - 16.0 * m1 + 30.0 * value - 16.0 * p1 + p2)
            sides = rim(
                before[x, b : b + 1, :] * flags[1],
                before[x, blocks + b : blocks + b + 1, :] * flags[1],
                after[x, b : b + 1, :] * flags[2],
                after[x, blocks + b : blocks + b + 1, :] * flags[2],
            )
            parts.append(stencil + sides + product[:, x * bs : (x + 1) * bs])
        vector = [outer[0, rows, :], outer[1, rows, :]]
        if column:
            parts = advance(
                parts[0], parts[1], [(o[0, rows, :], o[1, rows, :]) for o in old_image]
            )
            vector = advance(
                vector[0], vector[1], [(o[0, rows, :], o[1, rows, :]) for o in old_outer]
            )
            for x in range(2):
                new_outer[x, rows, :] = vector[x]
        result = []
        none = jnp.zeros((1, bs), jnp.float32)
        for x in range(2):
            if not last_step:
                image[x, rows, :] = parts[x]
            value = parts[x] + rim(
                new_ghost[x, blocks + b : blocks + b + 1, :] * flags[0],
                new_ghost[x, b : b + 1, :] * flags[0],
                none,
                none,
            )
            if not last_step:
                applied[x, rows, :] = value
            result.append(value)
        for k in range(count):
            if k < column:
                own = [old_outer[k][x, rows, :] for x in range(2)]
            else:
                own = vector
            reals[k] = reals[k] + tile_sum(own[0] * result[0] + own[1] * result[1])
            imags[k] = imags[k] + tile_sum(own[0] * result[1] - own[1] * result[0])
        square = square + tile_sum(vector[0] * vector[0] + vector[1] * vector[1])

    scalars = []
    w_real, w_imag = (applied_inner[0:1], applied_inner[1:2])
    for k in range(count):
        ref = old_inner[k] if k < column else new_inner
        u_real, u_imag = (ref[0:1], ref[1:2])
        scalars.append(full_sum(reals[k]) + full_sum(u_real * w_real + u_imag * w_imag))
        scalars.append(full_sum(imags[k]) + full_sum(u_real * w_imag - u_imag * w_real))
    scalars.append(full_sum(square) + full_sum(new_inner[...] * new_inner[...]))
    if last_step:
        ghost_out[...] = jnp.zeros_like(ghost_out)
        put_scalars(scalars, ghost_out, at_row)
    else:
        pack(
            applied,
            applied_inner[...],
            surface,
            flags,
            scalars,
            ghost_out,
            first_out,
            last_out,
            edge_out,
        )


def propagate(hess):
    scaled_block = jnp.zeros((2 * ITERS, 2 * ITERS), jnp.float32)
    for (i, j), (real, imag) in hess.items():
        for value, places in (
            (imag, ((i, j, 1.0), (i + ITERS, j + ITERS, 1.0))),
            (real, ((i, j + ITERS, 1.0), (i + ITERS, j, -1.0))),
        ):
            mask = np.zeros((2 * ITERS, 2 * ITERS), np.float32)
            for a, b, sign in places:
                mask[a, b] = sign
            scaled_block = scaled_block + (time_step * value) * mask
    scaled_block = scaled_block / 2.0**squarings
    identity = jnp.eye(2 * ITERS, dtype=jnp.float32)
    series = identity
    for degree in range(taylor_terms, 0, -1):
        series = identity + jnp.dot(scaled_block, series, precision=highest) / degree
    for repeat in range(squarings):
        series = jnp.dot(series, series, precision=highest)
    return (series[:ITERS, 0], series[ITERS:, 0])


def per_device(
    dims,
    outer_wave,
    inner_wave,
    surface,
    energies,
    coefficients,
    block_cols,
    block_kind,
    polarisation,
    laser_field,
):
    sec_index = lax.axis_index("sec")
    ch_index = lax.axis_index("ch")
    ch_count = lax.axis_size("ch")
    ch_dev = outer_wave.shape[1]
    rad_dev = outer_wave.shape[2]
    block_size = coefficients.shape[2]
    rows_dev = coefficients.shape[0]
    positions = sec_index * rad_dev + jnp.arange(rad_dev, dtype=jnp.int32)
    radius = inner_radius + (positions + 1).astype(jnp.float32) * grid_step
    first_sector = (sec_index == 0).astype(jnp.float32)
    last_sector = (sec_index == lax.axis_size("sec") - 1).astype(jnp.float32)
    local_cols = lax.dynamic_slice_in_dim(block_cols, ch_index * rows_dev, rows_dev, 0)
    local_kind = lax.dynamic_slice_in_dim(block_kind, ch_index * rows_dev, rows_dev, 0)
    local_polar = lax.dynamic_slice_in_dim(polarisation, ch_index * rows_dev, rows_dev, 0)
    local_factor = radial_factor(local_kind, local_polar, laser_field, radius)
    flags = jnp.stack([first_sector, 1.0 - first_sector, 1.0 - last_sector])
    shape = functools.partial(jax.ShapeDtypeStruct, dtype=jnp.float32)
    vmem = pl.BlockSpec(memory_space=pltpu.VMEM)
    smem = pl.BlockSpec(memory_space=pltpu.SMEM)
    params = pltpu.CompilerParams(vmem_limit_bytes=56 * 1024 * 1024)
    side = shape((2, 8, 128))
    packed = [shape((ch_count, 2, 8, 128)), side, side, side]
    outer_shape, inner_shape = (shape(outer_wave.shape), shape(inner_wave.shape))

    def swap(vector, payload):
        ghost_part, first, last, edge = [value.reshape(-1, 16, 128) for value in payload]
        sums, edges, before, after, full = exchange(
            dims, ghost_part, edge[0], first[0], last[0], vector
        )
        return (
            sums.reshape(2, 8, 128),
            edges.reshape(ch_count, 2, 8, 128),
            before.reshape(2, 8, 128),
            after.reshape(2, 8, 128),
            full,
        )

    payload = pl.pallas_call(
        prepare_kernel,
        out_shape=packed,
        in_specs=[smem] + [vmem] * 3,
        out_specs=[vmem] * 4,
        compiler_params=params,
        name="prepare",
    )(flags, outer_wave, inner_wave, surface)
    applied, applied_inner = (outer_wave, inner_wave)
    history, outers, inners, images, image_inners, ghosts, rims = ([], [], [], [], [], [], [])
    for column in range(ITERS):
        last_step = column + 1 == ITERS
        sums, edges, before, after, full = swap(applied, payload)
        args = [local_cols, flags, local_factor, coefficients, surface, energies[None]]
        args += [applied, applied_inner, sums, edges, before, after, full]
        args += history + outers + inners + images + image_inners + ghosts + rims
        outs = []
        if column:
            outs += [outer_shape, inner_shape, side, shape((ch_count, 2, 8, 128))]
        outs += [outer_shape, inner_shape, outer_shape, inner_shape]
        outs += packed[:1] if last_step else packed
        results = list(
            pl.pallas_call(
                functools.partial(step_kernel, column, last_step),
                out_shape=outs,
                in_specs=[smem, smem] + [vmem] * (len(args) - 2),
                out_specs=[vmem] * len(outs),
                scratch_shapes=[pltpu.VMEM((2, 8, ch_count * ch_dev), jnp.float32)],
                compiler_params=params,
                name="step",
            )(*args)
        )
        if column:
            new = results[:4]
            results = results[4:]
        else:
            new = [applied, applied_inner, sums, edges]
        for store, value in zip((outers, inners, ghosts, rims), new):
            store.append(value)
        history.append(sums)
        image, image_inner, applied, applied_inner = results[:4]
        images.append(image)
        image_inners.append(image_inner)
        payload = results[4:]
    last_rows = payload[0][:, 0]
    history.append(exchange(dims, last_rows)[0][None])
    rows = [value[0, 2 * rows_dev] for value in history]
    norms = [jnp.sqrt(rows[0][0] + 1e-06)]
    hess = {}
    for column in range(ITERS):
        totals = rows[column + 1]
        if column:
            norms.append(jnp.sqrt(totals[2 * column + 2] + 1e-06))
            hess[column, column - 1] = (norms[column], jnp.zeros((), jnp.float32))
        for row in range(column + 1):
            scale = 1.0 / (norms[row] * norms[column])
            hess[row, column] = (totals[2 * row] * scale, totals[2 * row + 1] * scale)
    coef_real, coef_imag = propagate(hess)
    outputs = []
    for store in (outers, inners):
        real, imag = (0.0, 0.0)
        for column in range(ITERS):
            scale = norms[0] / norms[column]
            part_real, part_imag = (coef_real[column] * scale, coef_imag[column] * scale)
            value = store[column]
            real = real + (part_real * value[0] - part_imag * value[1])
            imag = imag + (part_real * value[1] + part_imag * value[0])
        outputs.append(jnp.stack([real, imag]))
    return tuple(outputs)


def solution(mesh):
    placed = (
        P(None, "ch", "sec"),
        P(None, ("sec", "ch")),
        P(None, ("sec", "ch"), None),
        P(("sec", "ch")),
        P("ch", None, None, None),
        P(),
        P(),
        P(),
        P(),
    )
    return jax.shard_map(
        functools.partial(per_device, (8, 8, 2, 4)),
        mesh=mesh,
        in_specs=placed,
        out_specs=(P(None, "ch", "sec"), P(None, ("sec", "ch"))),
        check_vma=False,
    )
```

```python
import functools

import jax
import jax.numpy as jnp
from jax import lax
from jax.experimental import pallas as pl
from jax.experimental.pallas import tpu as pltpu
from jax.sharding import PartitionSpec as P

ITERS = 4


inner_radius = 20.0
grid_step = 0.08
time_step = 0.01
stencil_scale = 1.0 / (24.0 * grid_step * grid_step)
taylor_terms = 10
squarings = 7
highest = lax.Precision.HIGHEST


def radial_factor(kind_map, polar_map, laser_field, radius):
    radius_ratio = inner_radius / radius
    dipole_like = radius_ratio * radius_ratio
    quadrupole_like = dipole_like * radius_ratio
    chosen = jnp.sum(
        jnp.where(polar_map[..., None] == jnp.arange(3, dtype=jnp.int32), laser_field, 0.0), axis=-1
    )
    laser_term = chosen[..., None] * radius
    kind_wide = kind_map[..., None]
    return jnp.where(
        kind_wide == 0, dipole_like, jnp.where(kind_wide == 1, quadrupole_like, laser_term)
    )


MESH = pl.DeviceIdType.MESH


def exchange_kernel(dims, bulk, *refs):
    y_size, z_size, c_size, x_size = dims
    if bulk:
        (ghost_in, edge_in, first_in, last_in, outer_in) = refs[:5]
        (sum_out, edge_out, before_out, after_out, full_out) = refs[5:10]
        refs = refs[10:]
    else:
        (ghost_in, sum_out) = refs[:2]
        refs = refs[2:]
    (x_slots, c_slots, z_slots, y_slots) = refs[:4]
    (x_send, x_recv, c_send, c_recv, z_send, z_recv, y_send, y_recv) = refs[4:12]
    if bulk:
        (bulk_send, bulk_recv, side_send, side_recv, edge_send, edge_recv, own_sem) = refs[12:]
    sec = lax.axis_index("sec")
    x = lax.axis_index("ch")
    c = lax.rem(sec, c_size)
    z = lax.rem(sec // c_size, z_size)
    y = sec // (c_size * z_size)
    sec_size = y_size * z_size * c_size
    rows = ghost_in.shape[1]

    def x_peer(d):
        return {"ch": lax.rem(x + d, x_size)}

    def c_peer(d):
        return {"sec": (y * z_size + z) * c_size + lax.rem(c + d, c_size)}

    def z_peer(d):
        return {"sec": (y * z_size + lax.rem(z + d, z_size)) * c_size + c}

    def y_peer(d):
        return {"sec": (lax.rem(y + d, y_size) * z_size + z) * c_size + c}

    up = {"sec": lax.rem(sec + 1, sec_size)}
    down = {"sec": lax.rem(sec + sec_size - 1, sec_size)}

    greeted = []
    for size, peer in ((x_size, x_peer), (c_size, c_peer), (z_size, z_peer), (y_size, y_peer)):
        greeted += [peer(d) for d in range(1, size)]
    if bulk:
        greeted += [up, down]
    barrier = pltpu.get_barrier_semaphore()
    for peer in greeted:
        pl.semaphore_signal(barrier, inc=1, device_id=peer, device_id_type=MESH)
    pl.semaphore_wait(barrier, len(greeted))

    def remote(src, dst, send, recv, peer):
        copy = pltpu.make_async_remote_copy(
            src_ref=src,
            dst_ref=dst,
            send_sem=send,
            recv_sem=recv,
            device_id=peer,
            device_id_type=MESH,
        )
        copy.start()
        return copy

    x_copies = []
    for d in range(1, x_size):
        x_copies.append(
            remote(
                ghost_in.at[lax.rem(x + d, x_size)],
                x_slots.at[x],
                x_send.at[d - 1],
                x_recv.at[d - 1],
                x_peer(d),
            )
        )
    later = []
    if bulk:
        later.append(remote(last_in, before_out, side_send.at[0], side_recv.at[0], up))
        later.append(remote(first_in, after_out, side_send.at[1], side_recv.at[1], down))
        near = []
        for d in range(1, x_size):
            if x_size == 4 and d == 2:
                continue
            near.append(
                remote(
                    outer_in, full_out.at[x], bulk_send.at[d - 1], bulk_recv.at[d - 1], x_peer(d)
                )
            )
        own = pltpu.make_async_copy(outer_in, full_out.at[x], own_sem)
        own.start()
        later.append(own)
    x_slots[x] = ghost_in[x]
    for copy in x_copies:
        copy.wait()

    def total(slots, size):
        value = slots[0]
        for k in range(1, size):
            value = value + slots[k]
        return value

    c_slots[c, 0:rows] = total(x_slots, x_size)
    if bulk:
        c_slots[c, rows:] = edge_in[...]

    def stage(slots, me, size, peer, send, recv):
        copies = []
        for d in range(1, size):
            copies.append(
                remote(slots.at[me], slots.at[me], send.at[d - 1], recv.at[d - 1], peer(d))
            )
        for copy in copies:
            copy.wait()
        return total(slots, size)

    z_slots[z] = stage(c_slots, c, c_size, c_peer, c_send, c_recv)
    y_slots[y] = stage(z_slots, z, z_size, z_peer, z_send, z_recv)
    if bulk:
        for copy in near:
            copy.wait()
        if x_size == 4:
            for half, d, sem in ((0, 1, 1), (1, 3, 3)):
                held = full_out.at[lax.rem(x + x_size - d, x_size), half]
                later.append(remote(held, held, bulk_send.at[sem], bulk_recv.at[sem], x_peer(d)))
    value = stage(y_slots, y, y_size, y_peer, y_send, y_recv)
    sum_out[...] = value[0:rows]
    if bulk:
        edge_out[x] = value[rows:]
        copies = []
        for d in range(1, x_size):
            copies.append(
                remote(
                    edge_out.at[x],
                    edge_out.at[x],
                    edge_send.at[d - 1],
                    edge_recv.at[d - 1],
                    x_peer(d),
                )
            )
        for copy in copies + later:
            copy.wait()


def exchange(dims, ghosts, edges=None, first=None, last=None, outer=None):
    bulk = outer is not None
    y_size, z_size, c_size, x_size = dims
    x_count, rows, lanes = ghosts.shape
    vmem = pl.BlockSpec(memory_space=pltpu.VMEM)
    hbm = pl.BlockSpec(memory_space=pl.ANY)
    shape = functools.partial(jax.ShapeDtypeStruct, dtype=jnp.float32)
    outs = [shape((rows, lanes))]
    args = [ghosts]
    width = rows
    if bulk:
        args += [edges, first, last, outer]
        side = edges.shape
        width = rows + side[0]
        outs += [shape((x_size,) + side), shape(side), shape(side), shape((x_size,) + outer.shape)]
    dma = pltpu.SemaphoreType.DMA
    scratch = [
        pltpu.VMEM((x_size, rows, lanes), jnp.float32),
        pltpu.VMEM((c_size, width, lanes), jnp.float32),
        pltpu.VMEM((z_size, width, lanes), jnp.float32),
        pltpu.VMEM((y_size, width, lanes), jnp.float32),
    ]
    for size in (x_size, c_size, z_size, y_size):
        scratch += [dma((max(size - 1, 1),)), dma((max(size - 1, 1),))]
    if bulk:
        scratch += [dma((x_size,)), dma((x_size,)), dma((2,)), dma((2,))]
        scratch += [dma((x_size - 1,)), dma((x_size - 1,)), dma]
    return pl.pallas_call(
        functools.partial(exchange_kernel, dims, bulk),
        out_shape=outs,
        in_specs=[vmem] * len(args),
        out_specs=[vmem] * 4 + [hbm] if bulk else [vmem],
        scratch_shapes=scratch,
        compiler_params=pltpu.CompilerParams(collective_id=1 if bulk else 2, has_side_effects=True),
        name="exchange_bulk" if bulk else "exchange_sums",
    )(*args)


def exact_dot(a, b, dims=((1,), (0,))):
    return lax.dot_general(
        a, b, (dims, ((), ())), precision=highest, preferred_element_type=jnp.float32
    )


def full_sum(value):
    return jnp.sum(jnp.sum(value, axis=0, keepdims=True), axis=1, keepdims=True)


def tile_sum(value):
    return jnp.sum(value.reshape(value.shape[0] // 8, 8, value.shape[1]), axis=0)


def combine(scale, real, imag, terms):
    real, imag = (scale * real, scale * imag)
    for coef_real, coef_imag, other_real, other_imag in terms:
        real = real - (coef_real * other_real - coef_imag * other_imag)
        imag = imag - (coef_real * other_imag + coef_imag * other_real)
    return (real, imag)


def pick(row, k):
    lane = lax.broadcasted_iota(jnp.int32, row.shape, 1)
    return jnp.sum(jnp.where(lane == k, row, 0.0), axis=1, keepdims=True)


def pack(outer, inner, surface, flags, scalars, ghost_out, first_out, last_out, edge_out):
    ch_count = ghost_out.shape[0]
    bs = outer.shape[2]
    blocks = outer.shape[1] // bs
    ghost_out[...] = jnp.zeros_like(ghost_out)
    first_out[...] = jnp.zeros_like(first_out)
    last_out[...] = jnp.zeros_like(last_out)
    row_at = lax.broadcasted_iota(jnp.int32, (8, bs), 0)
    lane_at = lax.broadcasted_iota(jnp.int32, (8, bs), 1)
    wanted = jnp.where(row_at < 2, row_at, jnp.where(row_at < 4, row_at + bs - 4, -1))
    select = (lane_at == wanted).astype(jnp.float32)
    for x in range(2):
        for b in range(blocks):
            rows = exact_dot(select, outer[x, b * bs : (b + 1) * bs, :], ((1,), (1,)))
            for pt in range(2):
                at = pt * blocks + b
                first_out[x, at : at + 1, :] = rows[pt : pt + 1]
                last_out[x, at : at + 1, :] = rows[pt + 2 : pt + 3]
    edge_out[...] = first_out[...] * flags[0]
    for layer in range(2):
        sums = exact_dot(inner, surface[layer])
        for x in range(2):
            for p in range(ch_count):
                for b in range(blocks):
                    at, start = (layer * blocks + b, (p * blocks + b) * bs)
                    ghost_out[p, x, at : at + 1, :] = sums[x : x + 1, start : start + bs]
    put_scalars(scalars, ghost_out, 2 * blocks)


def put_scalars(scalars, ghost_out, at):
    lane = lax.broadcasted_iota(jnp.int32, (1, 128), 1)
    row = jnp.zeros((1, 128), jnp.float32)
    for k, value in enumerate(scalars):
        row = jnp.where(lane == k, value, row)
    for p in range(ghost_out.shape[0]):
        ghost_out[p, 0, at : at + 1, :] = row


def prepare_kernel(flags, outer, inner, surface, ghost_out, first_out, last_out, edge_out):
    value = full_sum(inner[...] * inner[...])
    for x in range(2):
        part = outer[x]
        value = value + full_sum(tile_sum(part * part))
    pack(outer, inner[...], surface, flags, [value], ghost_out, first_out, last_out, edge_out)


def step_kernel(column, last_step, *refs):
    refs = list(refs)
    take = lambda count: [refs.pop(0) for _ in range(count)]
    cols, flags, factor, coef, surface, energies = take(6)
    outer, inner, sums, edges, before, after, full = take(7)
    olds_sums = take(column)
    old_outer, old_inner = (take(column), take(column))
    old_image, old_image_inner = (take(column), take(column))
    old_ghost, old_edge = (take(column), take(column))
    if column:
        new_outer, new_inner, new_ghost, new_edge = take(4)
    else:
        new_outer, new_inner, new_ghost, new_edge = (outer, inner, sums, edges)
    image, image_inner, applied, applied_inner = take(4)
    if last_step:
        (ghost_out,) = take(1)
    else:
        ghost_out, first_out, last_out, edge_out = take(4)
    mixed = take(1)[0]
    bs = outer.shape[2]
    blocks = outer.shape[1] // bs
    slots = coef.shape[1]
    ch_count = edges.shape[0]
    at_row = 2 * blocks

    terms = []
    inverse = None
    if column:
        history = [ref[0, at_row : at_row + 1, :] for ref in olds_sums]
        history.append(sums[0, at_row : at_row + 1, :])
        roots = [lax.rsqrt(pick(history[0], 0) + 1e-06)]
        for k in range(1, column):
            roots.append(lax.rsqrt(pick(history[k + 1], 2 * k + 2) + 1e-06))
        inverse = roots[column - 1]
        for row in range(column):
            scale = roots[row] * roots[row] * inverse
            terms.append(
                (pick(history[column], 2 * row) * scale, pick(history[column], 2 * row + 1) * scale)
            )

    def advance(real, imag, others):
        return combine(
            inverse, real, imag, [t + o for t, o in zip(terms, others)]
        )

    if column:
        real, imag = advance(sums[0], sums[1], [(o[0], o[1]) for o in old_ghost])
        new_ghost[0] = real
        new_ghost[1] = imag
        for p in range(ch_count):
            real, imag = advance(edges[p, 0], edges[p, 1], [(o[p, 0], o[p, 1]) for o in old_edge])
            new_edge[p, 0] = real
            new_edge[p, 1] = imag
        real, imag = advance(
            inner[0:1], inner[1:2], [(o[0:1], o[1:2]) for o in old_inner]
        )
        new_inner[0:1] = real
        new_inner[1:2] = imag
        real, imag = advance(
            energies[...] * inner[0:1],
            energies[...] * inner[1:2],
            [(o[0:1], o[1:2]) for o in old_image_inner],
        )
        image_inner[0:1] = real
        image_inner[1:2] = imag
    else:
        image_inner[...] = energies[...] * inner[...]

    mixed[...] = jnp.zeros_like(mixed)
    for p in range(ch_count):
        for x in range(2):
            for b in range(blocks):
                start = (p * blocks + b) * bs
                zero = new_edge[p, x, b : b + 1, :]
                one = new_edge[p, x, blocks + b : blocks + b + 1, :]
                mixed[0, x : x + 1, start : start + bs] = -16.0 * zero + one
                mixed[1, x : x + 1, start : start + bs] = zero
    added = exact_dot(mixed[0], surface[0], ((1,), (1,)))
    added = added + exact_dot(mixed[1], surface[1], ((1,), (1,)))
    applied_inner[...] = image_inner[...] + stencil_scale * added[0:2]

    row_at = lax.broadcasted_iota(jnp.int32, (8, bs), 0)
    lane_at = lax.broadcasted_iota(jnp.int32, (8, bs), 1)

    def weight(row, lane, value):
        return jnp.where((row_at == row) & (lane_at == lane), value * stencil_scale, 0.0)

    weights = (
        weight(0, 0, 1.0)
        + weight(1, 0, -16.0)
        + weight(1, 1, 1.0)
        + weight(2, bs - 1, -16.0)
        + weight(2, bs - 2, 1.0)
        + weight(3, bs - 1, 1.0)
    )
    zeros = jnp.zeros((4, bs), jnp.float32)
    lane = lax.broadcasted_iota(jnp.int32, (bs, bs), 1)

    def rim(far, near, next0, next1):
        rows = jnp.concatenate([far, near, next0, next1, zeros], axis=0)
        return exact_dot(rows, weights, ((0,), (0,)))

    count = column + 1
    reals = [jnp.zeros((8, bs), jnp.float32) for _ in range(count)]
    imags = [jnp.zeros((8, bs), jnp.float32) for _ in range(count)]
    square = jnp.zeros((8, bs), jnp.float32)
    for b in range(blocks):
        rows = slice(b * bs, (b + 1) * bs)
        product = jnp.zeros((bs, 2 * bs), jnp.float32)
        for s in range(0, slots, 2):
            sides = []
            for t in (s, s + 1):
                col = cols[b, t]
                place = pl.ds(pl.multiple_of(lax.rem(col, blocks) * bs, bs), bs)
                owner = lax.div(col, blocks)
                scale = factor[b, t : t + 1, :]
                sides.append(
                    jnp.concatenate(
                        [full[owner, 0, place, :] * scale, full[owner, 1, place, :] * scale], axis=1
                    )
                )
            left = jnp.concatenate([coef[b, s], coef[b, s + 1]], axis=1)
            product = product + exact_dot(left, jnp.concatenate(sides, axis=0))
        parts = []
        for x in range(2):
            value = outer[x, rows, :]
            m1 = jnp.where(lane >= 1, pltpu.roll(value, 1, 1), 0.0)
            m2 = jnp.where(lane >= 2, pltpu.roll(value, 2, 1), 0.0)
            p1 = jnp.where(lane < bs - 1, pltpu.roll(value, bs - 1, 1), 0.0)
            p2 = jnp.where(lane < bs - 2, pltpu.roll(value, bs - 2, 1), 0.0)
            stencil = stencil_scale * (m2 - 16.0 * m1 + 30.0 * value - 16.0 * p1 + p2)
            sides = rim(
                before[x, b : b + 1, :] * flags[1],
                before[x, blocks + b : blocks + b + 1, :] * flags[1],
                after[x, b : b + 1, :] * flags[2],
                after[x, blocks + b : blocks + b + 1, :] * flags[2],
            )
            parts.append(stencil + sides + product[:, x * bs : (x + 1) * bs])
        vector = [outer[0, rows, :], outer[1, rows, :]]
        if column:
            parts = advance(
                parts[0], parts[1], [(o[0, rows, :], o[1, rows, :]) for o in old_image]
            )
            vector = advance(
                vector[0], vector[1], [(o[0, rows, :], o[1, rows, :]) for o in old_outer]
            )
            for x in range(2):
                new_outer[x, rows, :] = vector[x]
        result = []
        none = jnp.zeros((1, bs), jnp.float32)
        for x in range(2):
            if not last_step:
                image[x, rows, :] = parts[x]
            value = parts[x] + rim(
                new_ghost[x, blocks + b : blocks + b + 1, :] * flags[0],
                new_ghost[x, b : b + 1, :] * flags[0],
                none,
                none,
            )
            if not last_step:
                applied[x, rows, :] = value
            result.append(value)
        for k in range(count):
            if k < column:
                own = [old_outer[k][x, rows, :] for x in range(2)]
            else:
                own = vector
            reals[k] = reals[k] + tile_sum(own[0] * result[0] + own[1] * result[1])
            imags[k] = imags[k] + tile_sum(own[0] * result[1] - own[1] * result[0])
        square = square + tile_sum(vector[0] * vector[0] + vector[1] * vector[1])

    scalars = []
    w_real, w_imag = (applied_inner[0:1], applied_inner[1:2])
    for k in range(count):
        ref = old_inner[k] if k < column else new_inner
        u_real, u_imag = (ref[0:1], ref[1:2])
        scalars.append(full_sum(reals[k]) + full_sum(u_real * w_real + u_imag * w_imag))
        scalars.append(full_sum(imags[k]) + full_sum(u_real * w_imag - u_imag * w_real))
    scalars.append(full_sum(square) + full_sum(new_inner[...] * new_inner[...]))
    if last_step:
        ghost_out[...] = jnp.zeros_like(ghost_out)
        put_scalars(scalars, ghost_out, at_row)
    else:
        pack(
            applied,
            applied_inner[...],
            surface,
            flags,
            scalars,
            ghost_out,
            first_out,
            last_out,
            edge_out,
        )


def small_product(a, b):
    value = a[:, 0:1] * b[0:1, :]
    for k in range(1, 2 * ITERS):
        value = value + a[:, k : k + 1] * b[k : k + 1, :]
    return value


def finish_kernel(at_row, *refs):
    history = [ref[0, at_row : at_row + 1, :] for ref in refs[:ITERS]]
    history.append(refs[ITERS][at_row : at_row + 1, :])
    outers, inners = (refs[ITERS + 1 : 2 * ITERS + 1], refs[2 * ITERS + 1 : 3 * ITERS + 1])
    outer_out, inner_out = refs[3 * ITERS + 1 :]
    squares = [pick(history[0], 0) + 1e-06]
    for k in range(1, ITERS):
        squares.append(pick(history[k + 1], 2 * k + 2) + 1e-06)
    roots = [lax.rsqrt(value) for value in squares]
    row_at = lax.broadcasted_iota(jnp.int32, (2 * ITERS, 128), 0)
    lane_at = lax.broadcasted_iota(jnp.int32, (2 * ITERS, 128), 1)
    matrix = jnp.zeros((2 * ITERS, 128), jnp.float32)

    def put(value, i, j):
        return jnp.where((row_at == i) & (lane_at == j), value, matrix)

    for j in range(ITERS):
        for i in range(min(j + 2, ITERS)):
            if i <= j:
                scale = roots[i] * roots[j] * time_step
                real = pick(history[j + 1], 2 * i) * scale
                imag = pick(history[j + 1], 2 * i + 1) * scale
                matrix = put(imag, i, j)
                matrix = put(imag, i + ITERS, j + ITERS)
            else:
                real = jnp.sqrt(squares[i]) * time_step
            matrix = put(real, i, j + ITERS)
            matrix = put(-real, i + ITERS, j)
    matrix = matrix * (1.0 / 2.0**squarings)
    identity = jnp.where(row_at == lane_at, 1.0, 0.0)
    series = identity
    for degree in range(taylor_terms, 0, -1):
        series = identity + small_product(matrix, series) * (1.0 / degree)
    for repeat in range(squarings):
        series = small_product(series, series)
    terms = []
    start_norm = jnp.sqrt(squares[0])
    for j in range(ITERS):
        scale = start_norm * roots[j]
        terms.append((series[j : j + 1, 0:1] * scale, series[j + ITERS : j + ITERS + 1, 0:1] * scale))

    def total(values):
        real, imag = (0.0, 0.0)
        for (part_real, part_imag), (value_real, value_imag) in zip(terms, values):
            real = real + (part_real * value_real - part_imag * value_imag)
            imag = imag + (part_real * value_imag + part_imag * value_real)
        return (real, imag)

    inner_out[0:1], inner_out[1:2] = total([(ref[0:1], ref[1:2]) for ref in inners])
    bs = outer_out.shape[2]
    for b in range(outer_out.shape[1] // bs):
        rows = slice(b * bs, (b + 1) * bs)
        real, imag = total([(ref[0, rows, :], ref[1, rows, :]) for ref in outers])
        outer_out[0, rows, :] = real
        outer_out[1, rows, :] = imag


def per_device(
    dims,
    outer_wave,
    inner_wave,
    surface,
    energies,
    coefficients,
    block_cols,
    block_kind,
    polarisation,
    laser_field,
):
    sec_index = lax.axis_index("sec")
    ch_index = lax.axis_index("ch")
    ch_count = lax.axis_size("ch")
    ch_dev = outer_wave.shape[1]
    rad_dev = outer_wave.shape[2]
    block_size = coefficients.shape[2]
    rows_dev = coefficients.shape[0]
    positions = sec_index * rad_dev + jnp.arange(rad_dev, dtype=jnp.int32)
    radius = inner_radius + (positions + 1).astype(jnp.float32) * grid_step
    first_sector = (sec_index == 0).astype(jnp.float32)
    last_sector = (sec_index == lax.axis_size("sec") - 1).astype(jnp.float32)
    local_cols = lax.dynamic_slice_in_dim(block_cols, ch_index * rows_dev, rows_dev, 0)
    local_kind = lax.dynamic_slice_in_dim(block_kind, ch_index * rows_dev, rows_dev, 0)
    local_polar = lax.dynamic_slice_in_dim(polarisation, ch_index * rows_dev, rows_dev, 0)
    local_factor = radial_factor(local_kind, local_polar, laser_field, radius)
    flags = jnp.stack([first_sector, 1.0 - first_sector, 1.0 - last_sector])
    shape = functools.partial(jax.ShapeDtypeStruct, dtype=jnp.float32)
    vmem = pl.BlockSpec(memory_space=pltpu.VMEM)
    smem = pl.BlockSpec(memory_space=pltpu.SMEM)
    params = pltpu.CompilerParams(vmem_limit_bytes=56 * 1024 * 1024)
    side = shape((2, 8, 128))
    packed = [shape((ch_count, 2, 8, 128)), side, side, side]
    outer_shape, inner_shape = (shape(outer_wave.shape), shape(inner_wave.shape))

    def swap(vector, payload):
        ghost_part, first, last, edge = [value.reshape(-1, 16, 128) for value in payload]
        sums, edges, before, after, full = exchange(
            dims, ghost_part, edge[0], first[0], last[0], vector
        )
        return (
            sums.reshape(2, 8, 128),
            edges.reshape(ch_count, 2, 8, 128),
            before.reshape(2, 8, 128),
            after.reshape(2, 8, 128),
            full,
        )

    payload = pl.pallas_call(
        prepare_kernel,
        out_shape=packed,
        in_specs=[smem] + [vmem] * 3,
        out_specs=[vmem] * 4,
        compiler_params=params,
        name="prepare",
    )(flags, outer_wave, inner_wave, surface)
    applied, applied_inner = (outer_wave, inner_wave)
    history, outers, inners, images, image_inners, ghosts, rims = ([], [], [], [], [], [], [])
    for column in range(ITERS):
        last_step = column + 1 == ITERS
        sums, edges, before, after, full = swap(applied, payload)
        args = [local_cols, flags, local_factor, coefficients, surface, energies[None]]
        args += [applied, applied_inner, sums, edges, before, after, full]
        args += history + outers + inners + images + image_inners + ghosts + rims
        outs = []
        if column:
            outs += [outer_shape, inner_shape, side, shape((ch_count, 2, 8, 128))]
        outs += [outer_shape, inner_shape, outer_shape, inner_shape]
        outs += [shape((ch_count, 1, 8, 128))] if last_step else packed
        results = list(
            pl.pallas_call(
                functools.partial(step_kernel, column, last_step),
                out_shape=outs,
                in_specs=[smem, smem] + [vmem] * (len(args) - 2),
                out_specs=[vmem] * len(outs),
                scratch_shapes=[pltpu.VMEM((2, 8, ch_count * ch_dev), jnp.float32)],
                compiler_params=params,
                name="step",
            )(*args)
        )
        if column:
            new = results[:4]
            results = results[4:]
        else:
            new = [applied, applied_inner, sums, edges]
        for store, value in zip((outers, inners, ghosts, rims), new):
            store.append(value)
        history.append(sums)
        image, image_inner, applied, applied_inner = results[:4]
        images.append(image)
        image_inners.append(image_inner)
        payload = results[4:]
    last_sums = exchange(dims, payload[0].reshape(ch_count, 8, 128))[0]
    args = history + [last_sums] + outers + inners
    return tuple(
        pl.pallas_call(
            functools.partial(finish_kernel, 2 * rows_dev),
            out_shape=[outer_shape, inner_shape],
            in_specs=[vmem] * len(args),
            out_specs=[vmem] * 2,
            compiler_params=params,
            name="finish",
        )(*args)
    )


def solution(mesh):
    placed = (
        P(None, "ch", "sec"),
        P(None, ("sec", "ch")),
        P(None, ("sec", "ch"), None),
        P(("sec", "ch")),
        P("ch", None, None, None),
        P(),
        P(),
        P(),
        P(),
    )
    return jax.shard_map(
        functools.partial(per_device, (8, 8, 2, 4)),
        mesh=mesh,
        in_specs=placed,
        out_specs=(P(None, "ch", "sec"), P(None, ("sec", "ch"))),
        check_vma=False,
    )
```

```python
import functools

import jax
import jax.numpy as jnp
from jax import lax
from jax.experimental import pallas as pl
from jax.experimental.pallas import tpu as pltpu
from jax.sharding import PartitionSpec as P

ITERS = 4


inner_radius = 20.0
grid_step = 0.08
time_step = 0.01
stencil_scale = 1.0 / (24.0 * grid_step * grid_step)
taylor_terms = 10
squarings = 7
highest = lax.Precision.HIGHEST


def radial_factor(kind_map, polar_map, laser_field, radius):
    radius_ratio = inner_radius / radius
    dipole_like = radius_ratio * radius_ratio
    quadrupole_like = dipole_like * radius_ratio
    chosen = jnp.sum(
        jnp.where(polar_map[..., None] == jnp.arange(3, dtype=jnp.int32), laser_field, 0.0), axis=-1
    )
    laser_term = chosen[..., None] * radius
    kind_wide = kind_map[..., None]
    return jnp.where(
        kind_wide == 0, dipole_like, jnp.where(kind_wide == 1, quadrupole_like, laser_term)
    )


MESH = pl.DeviceIdType.MESH


def exchange_kernel(dims, bulk, *refs):
    y_size, z_size, c_size, x_size = dims
    if bulk:
        (ghost_in, edge_in, first_in, last_in, outer_in) = refs[:5]
        (sum_out, edge_out, before_out, after_out, full_out) = refs[5:10]
        refs = refs[10:]
    else:
        (ghost_in, sum_out) = refs[:2]
        refs = refs[2:]
    (x_slots, c_slots, z_slots, y_slots) = refs[:4]
    (x_send, x_recv, c_send, c_recv, z_send, z_recv, y_send, y_recv) = refs[4:12]
    if bulk:
        (bulk_send, bulk_recv, side_send, side_recv, edge_send, edge_recv, own_sem) = refs[12:19]
        (cross_send, pass_send, pass_recv, c_land) = refs[19:]
    sec = lax.axis_index("sec")
    x = lax.axis_index("ch")
    c = lax.rem(sec, c_size)
    z = lax.rem(sec // c_size, z_size)
    y = sec // (c_size * z_size)
    sec_size = y_size * z_size * c_size
    rows = ghost_in.shape[1]

    def x_peer(d):
        return {"ch": lax.rem(x + d, x_size)}

    def c_peer(d):
        return {"sec": (y * z_size + z) * c_size + lax.rem(c + d, c_size)}

    def z_peer(d):
        return {"sec": (y * z_size + lax.rem(z + d, z_size)) * c_size + c}

    def y_peer(d):
        return {"sec": (lax.rem(y + d, y_size) * z_size + z) * c_size + c}

    up = {"sec": lax.rem(sec + 1, sec_size)}
    down = {"sec": lax.rem(sec + sec_size - 1, sec_size)}

    greeted = []
    for size, peer in ((x_size, x_peer), (c_size, c_peer), (z_size, z_peer), (y_size, y_peer)):
        greeted += [peer(d) for d in range(1, size)]
    def cross_peer(d):
        return dict(x_peer(d), **c_peer(1))

    if bulk:
        greeted += [up, down]
        greeted += [cross_peer(d) for d in range(1, x_size)]
    barrier = pltpu.get_barrier_semaphore()
    for peer in greeted:
        pl.semaphore_signal(barrier, inc=1, device_id=peer, device_id_type=MESH)
    pl.semaphore_wait(barrier, len(greeted))

    def remote(src, dst, send, recv, peer):
        copy = pltpu.make_async_remote_copy(
            src_ref=src,
            dst_ref=dst,
            send_sem=send,
            recv_sem=recv,
            device_id=peer,
            device_id_type=MESH,
        )
        copy.start()
        return copy

    x_copies = []
    for d in range(1, x_size):
        x_copies.append(
            remote(
                ghost_in.at[lax.rem(x + d, x_size)],
                x_slots.at[x],
                x_send.at[d - 1],
                x_recv.at[d - 1],
                x_peer(d),
            )
        )
    later = []
    if bulk:
        later.append(remote(last_in, before_out, side_send.at[0], side_recv.at[0], up))
        later.append(remote(first_in, after_out, side_send.at[1], side_recv.at[1], down))
        near = []
        for d in range(1, x_size):
            if x_size == 4 and d == 2:
                continue
            near.append(
                remote(
                    outer_in, full_out.at[x], bulk_send.at[d - 1], bulk_recv.at[d - 1], x_peer(d)
                )
            )
        own = pltpu.make_async_copy(outer_in, full_out.at[x], own_sem)
        own.start()
        later.append(own)
    x_slots[x] = ghost_in[x]
    for copy in x_copies:
        copy.wait()

    def total(slots, size):
        value = slots[0]
        for k in range(1, size):
            value = value + slots[k]
        return value

    if bulk:
        c_slots[0] = total(x_slots, x_size)
        c_slots[1] = edge_in[...]
    else:
        c_slots[c] = total(x_slots, x_size)

    def stage(slots, me, size, peer, send, recv):
        copies = []
        for d in range(1, size):
            copies.append(
                remote(slots.at[me], slots.at[me], send.at[d - 1], recv.at[d - 1], peer(d))
            )
        for copy in copies:
            copy.wait()
        return total(slots, size)

    if bulk:
        remote(c_slots.at[1 - c], c_land, c_send.at[0], c_recv.at[0], c_peer(1)).wait()
        z_slots[z] = c_slots[c] + c_land[...]
    else:
        z_slots[z] = stage(c_slots, c, c_size, c_peer, c_send, c_recv)
    y_slots[y] = stage(z_slots, z, z_size, z_peer, z_send, z_recv)
    if bulk:
        for copy in near:
            copy.wait()
        if x_size == 4:
            for half, d, sem in ((0, 1, 1), (1, 3, 3)):
                held = full_out.at[lax.rem(x + x_size - d, x_size), half]
                later.append(remote(held, held, bulk_send.at[sem], bulk_recv.at[sem], x_peer(d)))
    value = stage(y_slots, y, y_size, y_peer, y_send, y_recv)
    if not bulk:
        sum_out[...] = value
        return

    def pass_sums():
        return pltpu.make_async_remote_copy(
            src_ref=sum_out,
            dst_ref=sum_out,
            send_sem=pass_send,
            recv_sem=pass_recv,
            device_id=c_peer(1),
            device_id_type=MESH,
        )

    def edge_from(d):
        place = edge_out.at[lax.rem(x + x_size - d, x_size)]
        return pltpu.make_async_remote_copy(
            src_ref=place,
            dst_ref=place,
            send_sem=edge_send.at[d],
            recv_sem=edge_recv.at[d],
            device_id=cross_peer(d),
            device_id_type=MESH,
        )

    @pl.when(c == 0)
    def _():
        sum_out[...] = value
        copy = pass_sums()
        copy.start()
        copy.wait_send()
        for d in range(x_size):
            edge_from(d).wait_recv()

    @pl.when(c == 1)
    def _():
        edge_out[x] = value
        place = edge_out.at[x]
        copies = []
        across = []
        for d in range(x_size):
            across.append(
                remote(place, place, cross_send.at[d], edge_recv.at[d], cross_peer(d))
            )
            if d:
                copies.append(remote(place, place, edge_send.at[d], edge_recv.at[d], x_peer(d)))
        for copy in across:
            copy.wait_send()
        for copy in copies:
            copy.wait()
        pass_sums().wait_recv()

    for copy in later:
        copy.wait()


def exchange(dims, ghosts, edges=None, first=None, last=None, outer=None):
    bulk = outer is not None
    y_size, z_size, c_size, x_size = dims
    x_count, rows, lanes = ghosts.shape
    vmem = pl.BlockSpec(memory_space=pltpu.VMEM)
    hbm = pl.BlockSpec(memory_space=pl.ANY)
    shape = functools.partial(jax.ShapeDtypeStruct, dtype=jnp.float32)
    outs = [shape((rows, lanes))]
    args = [ghosts]
    width = rows
    if bulk:
        args += [edges, first, last, outer]
        side = edges.shape
        outs += [shape((x_size,) + side), shape(side), shape(side), shape((x_size,) + outer.shape)]
    dma = pltpu.SemaphoreType.DMA
    scratch = [
        pltpu.VMEM((x_size, rows, lanes), jnp.float32),
        pltpu.VMEM((c_size, width, lanes), jnp.float32),
        pltpu.VMEM((z_size, width, lanes), jnp.float32),
        pltpu.VMEM((y_size, width, lanes), jnp.float32),
    ]
    for size in (x_size, c_size, z_size, y_size):
        scratch += [dma((max(size - 1, 1),)), dma((max(size - 1, 1),))]
    if bulk:
        scratch += [dma((x_size,)), dma((x_size,)), dma((2,)), dma((2,))]
        scratch += [dma((x_size,)), dma((x_size,)), dma]
        scratch += [dma((x_size,)), dma, dma, pltpu.VMEM((rows, lanes), jnp.float32)]
    return pl.pallas_call(
        functools.partial(exchange_kernel, dims, bulk),
        out_shape=outs,
        in_specs=[vmem] * len(args),
        out_specs=[vmem] * 4 + [hbm] if bulk else [vmem],
        scratch_shapes=scratch,
        compiler_params=pltpu.CompilerParams(collective_id=1 if bulk else 2, has_side_effects=True),
        name="exchange_bulk" if bulk else "exchange_sums",
    )(*args)


def exact_dot(a, b, dims=((1,), (0,))):
    return lax.dot_general(
        a, b, (dims, ((), ())), precision=highest, preferred_element_type=jnp.float32
    )


def full_sum(value):
    return jnp.sum(jnp.sum(value, axis=0, keepdims=True), axis=1, keepdims=True)


def tile_sum(value):
    return jnp.sum(value.reshape(value.shape[0] // 8, 8, value.shape[1]), axis=0)


def combine(scale, real, imag, terms):
    real, imag = (scale * real, scale * imag)
    for coef_real, coef_imag, other_real, other_imag in terms:
        real = real - (coef_real * other_real - coef_imag * other_imag)
        imag = imag - (coef_real * other_imag + coef_imag * other_real)
    return (real, imag)


def pick(row, k):
    lane = lax.broadcasted_iota(jnp.int32, row.shape, 1)
    return jnp.sum(jnp.where(lane == k, row, 0.0), axis=1, keepdims=True)


def pack(outer, inner, surface, flags, scalars, ghost_out, first_out, last_out, edge_out):
    ch_count = ghost_out.shape[0]
    bs = outer.shape[2]
    blocks = outer.shape[1] // bs
    ghost_out[...] = jnp.zeros_like(ghost_out)
    first_out[...] = jnp.zeros_like(first_out)
    last_out[...] = jnp.zeros_like(last_out)
    row_at = lax.broadcasted_iota(jnp.int32, (8, bs), 0)
    lane_at = lax.broadcasted_iota(jnp.int32, (8, bs), 1)
    wanted = jnp.where(row_at < 2, row_at, jnp.where(row_at < 4, row_at + bs - 4, -1))
    select = (lane_at == wanted).astype(jnp.float32)
    for x in range(2):
        for b in range(blocks):
            rows = exact_dot(select, outer[x, b * bs : (b + 1) * bs, :], ((1,), (1,)))
            for pt in range(2):
                at = pt * blocks + b
                first_out[x, at : at + 1, :] = rows[pt : pt + 1]
                last_out[x, at : at + 1, :] = rows[pt + 2 : pt + 3]
    edge_out[...] = first_out[...] * flags[0]
    for layer in range(2):
        sums = exact_dot(inner, surface[layer])
        for x in range(2):
            for p in range(ch_count):
                for b in range(blocks):
                    at, start = (layer * blocks + b, (p * blocks + b) * bs)
                    ghost_out[p, x, at : at + 1, :] = sums[x : x + 1, start : start + bs]
    put_scalars(scalars, ghost_out, 2 * blocks)


def put_scalars(scalars, ghost_out, at):
    lane = lax.broadcasted_iota(jnp.int32, (1, 128), 1)
    row = jnp.zeros((1, 128), jnp.float32)
    for k, value in enumerate(scalars):
        row = jnp.where(lane == k, value, row)
    for p in range(ghost_out.shape[0]):
        ghost_out[p, 0, at : at + 1, :] = row


def prepare_kernel(flags, outer, inner, surface, ghost_out, first_out, last_out, edge_out):
    value = full_sum(inner[...] * inner[...])
    for x in range(2):
        part = outer[x]
        value = value + full_sum(tile_sum(part * part))
    pack(outer, inner[...], surface, flags, [value], ghost_out, first_out, last_out, edge_out)


def step_kernel(column, last_step, *refs):
    refs = list(refs)
    take = lambda count: [refs.pop(0) for _ in range(count)]
    cols, flags, factor, coef, surface, energies = take(6)
    outer, inner, sums, edges, before, after, full = take(7)
    olds_sums = take(column)
    old_outer, old_inner = (take(column), take(column))
    old_image, old_image_inner = (take(column), take(column))
    old_ghost, old_edge = (take(column), take(column))
    if column:
        new_outer, new_inner, new_ghost, new_edge = take(4)
    else:
        new_outer, new_inner, new_ghost, new_edge = (outer, inner, sums, edges)
    image, image_inner, applied, applied_inner = take(4)
    if last_step:
        (ghost_out,) = take(1)
    else:
        ghost_out, first_out, last_out, edge_out = take(4)
    mixed = take(1)[0]
    bs = outer.shape[2]
    blocks = outer.shape[1] // bs
    slots = coef.shape[1]
    ch_count = edges.shape[0]
    at_row = 2 * blocks

    terms = []
    inverse = None
    if column:
        history = [ref[0, at_row : at_row + 1, :] for ref in olds_sums]
        history.append(sums[0, at_row : at_row + 1, :])
        roots = [lax.rsqrt(pick(history[0], 0) + 1e-06)]
        for k in range(1, column):
            roots.append(lax.rsqrt(pick(history[k + 1], 2 * k + 2) + 1e-06))
        inverse = roots[column - 1]
        for row in range(column):
            scale = roots[row] * roots[row] * inverse
            terms.append(
                (pick(history[column], 2 * row) * scale, pick(history[column], 2 * row + 1) * scale)
            )

    def advance(real, imag, others):
        return combine(
            inverse, real, imag, [t + o for t, o in zip(terms, others)]
        )

    if column:
        real, imag = advance(sums[0], sums[1], [(o[0], o[1]) for o in old_ghost])
        new_ghost[0] = real
        new_ghost[1] = imag
        for p in range(ch_count):
            real, imag = advance(edges[p, 0], edges[p, 1], [(o[p, 0], o[p, 1]) for o in old_edge])
            new_edge[p, 0] = real
            new_edge[p, 1] = imag
        real, imag = advance(
            inner[0:1], inner[1:2], [(o[0:1], o[1:2]) for o in old_inner]
        )
        new_inner[0:1] = real
        new_inner[1:2] = imag
        real, imag = advance(
            energies[...] * inner[0:1],
            energies[...] * inner[1:2],
            [(o[0:1], o[1:2]) for o in old_image_inner],
        )
        image_inner[0:1] = real
        image_inner[1:2] = imag
    else:
        image_inner[...] = energies[...] * inner[...]

    mixed[...] = jnp.zeros_like(mixed)
    for p in range(ch_count):
        for x in range(2):
            for b in range(blocks):
                start = (p * blocks + b) * bs
                zero = new_edge[p, x, b : b + 1, :]
                one = new_edge[p, x, blocks + b : blocks + b + 1, :]
                mixed[0, x : x + 1, start : start + bs] = -16.0 * zero + one
                mixed[1, x : x + 1, start : start + bs] = zero
    added = exact_dot(mixed[0], surface[0], ((1,), (1,)))
    added = added + exact_dot(mixed[1], surface[1], ((1,), (1,)))
    applied_inner[...] = image_inner[...] + stencil_scale * added[0:2]

    row_at = lax.broadcasted_iota(jnp.int32, (8, bs), 0)
    lane_at = lax.broadcasted_iota(jnp.int32, (8, bs), 1)

    def weight(row, lane, value):
        return jnp.where((row_at == row) & (lane_at == lane), value * stencil_scale, 0.0)

    weights = (
        weight(0, 0, 1.0)
        + weight(1, 0, -16.0)
        + weight(1, 1, 1.0)
        + weight(2, bs - 1, -16.0)
        + weight(2, bs - 2, 1.0)
        + weight(3, bs - 1, 1.0)
    )
    zeros = jnp.zeros((4, bs), jnp.float32)
    lane = lax.broadcasted_iota(jnp.int32, (bs, bs), 1)

    def rim(far, near, next0, next1):
        rows = jnp.concatenate([far, near, next0, next1, zeros], axis=0)
        return exact_dot(rows, weights, ((0,), (0,)))

    count = column + 1
    reals = [jnp.zeros((8, bs), jnp.float32) for _ in range(count)]
    imags = [jnp.zeros((8, bs), jnp.float32) for _ in range(count)]
    square = jnp.zeros((8, bs), jnp.float32)
    for b in range(blocks):
        rows = slice(b * bs, (b + 1) * bs)
        product = jnp.zeros((bs, 2 * bs), jnp.float32)
        for s in range(0, slots, 2):
            sides = []
            for t in (s, s + 1):
                col = cols[b, t]
                place = pl.ds(pl.multiple_of(lax.rem(col, blocks) * bs, bs), bs)
                owner = lax.div(col, blocks)
                scale = factor[b, t : t + 1, :]
                sides.append(
                    jnp.concatenate(
                        [full[owner, 0, place, :] * scale, full[owner, 1, place, :] * scale], axis=1
                    )
                )
            left = jnp.concatenate([coef[b, s], coef[b, s + 1]], axis=1)
            product = product + exact_dot(left, jnp.concatenate(sides, axis=0))
        parts = []
        for x in range(2):
            value = outer[x, rows, :]
            m1 = jnp.where(lane >= 1, pltpu.roll(value, 1, 1), 0.0)
            m2 = jnp.where(lane >= 2, pltpu.roll(value, 2, 1), 0.0)
            p1 = jnp.where(lane < bs - 1, pltpu.roll(value, bs - 1, 1), 0.0)
            p2 = jnp.where(lane < bs - 2, pltpu.roll(value, bs - 2, 1), 0.0)
            stencil = stencil_scale * (m2 - 16.0 * m1 + 30.0 * value - 16.0 * p1 + p2)
            sides = rim(
                before[x, b : b + 1, :] * flags[1],
                before[x, blocks + b : blocks + b + 1, :] * flags[1],
                after[x, b : b + 1, :] * flags[2],
                after[x, blocks + b : blocks + b + 1, :] * flags[2],
            )
            parts.append(stencil + sides + product[:, x * bs : (x + 1) * bs])
        vector = [outer[0, rows, :], outer[1, rows, :]]
        if column:
            parts = advance(
                parts[0], parts[1], [(o[0, rows, :], o[1, rows, :]) for o in old_image]
            )
            vector = advance(
                vector[0], vector[1], [(o[0, rows, :], o[1, rows, :]) for o in old_outer]
            )
            for x in range(2):
                new_outer[x, rows, :] = vector[x]
        result = []
        none = jnp.zeros((1, bs), jnp.float32)
        for x in range(2):
            if not last_step:
                image[x, rows, :] = parts[x]
            value = parts[x] + rim(
                new_ghost[x, blocks + b : blocks + b + 1, :] * flags[0],
                new_ghost[x, b : b + 1, :] * flags[0],
                none,
                none,
            )
            if not last_step:
                applied[x, rows, :] = value
            result.append(value)
        for k in range(count):
            if k < column:
                own = [old_outer[k][x, rows, :] for x in range(2)]
            else:
                own = vector
            reals[k] = reals[k] + tile_sum(own[0] * result[0] + own[1] * result[1])
            imags[k] = imags[k] + tile_sum(own[0] * result[1] - own[1] * result[0])
        square = square + tile_sum(vector[0] * vector[0] + vector[1] * vector[1])

    scalars = []
    w_real, w_imag = (applied_inner[0:1], applied_inner[1:2])
    for k in range(count):
        ref = old_inner[k] if k < column else new_inner
        u_real, u_imag = (ref[0:1], ref[1:2])
        scalars.append(full_sum(reals[k]) + full_sum(u_real * w_real + u_imag * w_imag))
        scalars.append(full_sum(imags[k]) + full_sum(u_real * w_imag - u_imag * w_real))
    scalars.append(full_sum(square) + full_sum(new_inner[...] * new_inner[...]))
    if last_step:
        ghost_out[...] = jnp.zeros_like(ghost_out)
        put_scalars(scalars, ghost_out, at_row)
    else:
        pack(
            applied,
            applied_inner[...],
            surface,
            flags,
            scalars,
            ghost_out,
            first_out,
            last_out,
            edge_out,
        )


def small_product(a, b):
    value = a[:, 0:1] * b[0:1, :]
    for k in range(1, 2 * ITERS):
        value = value + a[:, k : k + 1] * b[k : k + 1, :]
    return value


def finish_kernel(at_row, *refs):
    history = [ref[0, at_row : at_row + 1, :] for ref in refs[:ITERS]]
    history.append(refs[ITERS][at_row : at_row + 1, :])
    outers, inners = (refs[ITERS + 1 : 2 * ITERS + 1], refs[2 * ITERS + 1 : 3 * ITERS + 1])
    outer_out, inner_out = refs[3 * ITERS + 1 :]
    squares = [pick(history[0], 0) + 1e-06]
    for k in range(1, ITERS):
        squares.append(pick(history[k + 1], 2 * k + 2) + 1e-06)
    roots = [lax.rsqrt(value) for value in squares]
    row_at = lax.broadcasted_iota(jnp.int32, (2 * ITERS, 128), 0)
    lane_at = lax.broadcasted_iota(jnp.int32, (2 * ITERS, 128), 1)
    matrix = jnp.zeros((2 * ITERS, 128), jnp.float32)

    def put(value, i, j):
        return jnp.where((row_at == i) & (lane_at == j), value, matrix)

    for j in range(ITERS):
        for i in range(min(j + 2, ITERS)):
            if i <= j:
                scale = roots[i] * roots[j] * time_step
                real = pick(history[j + 1], 2 * i) * scale
                imag = pick(history[j + 1], 2 * i + 1) * scale
                matrix = put(imag, i, j)
                matrix = put(imag, i + ITERS, j + ITERS)
            else:
                real = jnp.sqrt(squares[i]) * time_step
            matrix = put(real, i, j + ITERS)
            matrix = put(-real, i + ITERS, j)
    matrix = matrix * (1.0 / 2.0**squarings)
    identity = jnp.where(row_at == lane_at, 1.0, 0.0)
    series = identity
    for degree in range(taylor_terms, 0, -1):
        series = identity + small_product(matrix, series) * (1.0 / degree)
    for repeat in range(squarings):
        series = small_product(series, series)
    terms = []
    start_norm = jnp.sqrt(squares[0])
    for j in range(ITERS):
        scale = start_norm * roots[j]
        terms.append((series[j : j + 1, 0:1] * scale, series[j + ITERS : j + ITERS + 1, 0:1] * scale))

    def total(values):
        real, imag = (0.0, 0.0)
        for (part_real, part_imag), (value_real, value_imag) in zip(terms, values):
            real = real + (part_real * value_real - part_imag * value_imag)
            imag = imag + (part_real * value_imag + part_imag * value_real)
        return (real, imag)

    inner_out[0:1], inner_out[1:2] = total([(ref[0:1], ref[1:2]) for ref in inners])
    bs = outer_out.shape[2]
    for b in range(outer_out.shape[1] // bs):
        rows = slice(b * bs, (b + 1) * bs)
        real, imag = total([(ref[0, rows, :], ref[1, rows, :]) for ref in outers])
        outer_out[0, rows, :] = real
        outer_out[1, rows, :] = imag


def per_device(
    dims,
    outer_wave,
    inner_wave,
    surface,
    energies,
    coefficients,
    block_cols,
    block_kind,
    polarisation,
    laser_field,
):
    sec_index = lax.axis_index("sec")
    ch_index = lax.axis_index("ch")
    ch_count = lax.axis_size("ch")
    ch_dev = outer_wave.shape[1]
    rad_dev = outer_wave.shape[2]
    block_size = coefficients.shape[2]
    rows_dev = coefficients.shape[0]
    positions = sec_index * rad_dev + jnp.arange(rad_dev, dtype=jnp.int32)
    radius = inner_radius + (positions + 1).astype(jnp.float32) * grid_step
    first_sector = (sec_index == 0).astype(jnp.float32)
    last_sector = (sec_index == lax.axis_size("sec") - 1).astype(jnp.float32)
    local_cols = lax.dynamic_slice_in_dim(block_cols, ch_index * rows_dev, rows_dev, 0)
    local_kind = lax.dynamic_slice_in_dim(block_kind, ch_index * rows_dev, rows_dev, 0)
    local_polar = lax.dynamic_slice_in_dim(polarisation, ch_index * rows_dev, rows_dev, 0)
    local_factor = radial_factor(local_kind, local_polar, laser_field, radius)
    flags = jnp.stack([first_sector, 1.0 - first_sector, 1.0 - last_sector])
    shape = functools.partial(jax.ShapeDtypeStruct, dtype=jnp.float32)
    vmem = pl.BlockSpec(memory_space=pltpu.VMEM)
    smem = pl.BlockSpec(memory_space=pltpu.SMEM)
    params = pltpu.CompilerParams(vmem_limit_bytes=56 * 1024 * 1024)
    side = shape((2, 8, 128))
    packed = [shape((ch_count, 2, 8, 128)), side, side, side]
    outer_shape, inner_shape = (shape(outer_wave.shape), shape(inner_wave.shape))

    def swap(vector, payload):
        ghost_part, first, last, edge = [value.reshape(-1, 16, 128) for value in payload]
        sums, edges, before, after, full = exchange(
            dims, ghost_part, edge[0], first[0], last[0], vector
        )
        return (
            sums.reshape(2, 8, 128),
            edges.reshape(ch_count, 2, 8, 128),
            before.reshape(2, 8, 128),
            after.reshape(2, 8, 128),
            full,
        )

    payload = pl.pallas_call(
        prepare_kernel,
        out_shape=packed,
        in_specs=[smem] + [vmem] * 3,
        out_specs=[vmem] * 4,
        compiler_params=params,
        name="prepare",
    )(flags, outer_wave, inner_wave, surface)
    applied, applied_inner = (outer_wave, inner_wave)
    history, outers, inners, images, image_inners, ghosts, rims = ([], [], [], [], [], [], [])
    for column in range(ITERS):
        last_step = column + 1 == ITERS
        sums, edges, before, after, full = swap(applied, payload)
        args = [local_cols, flags, local_factor, coefficients, surface, energies[None]]
        args += [applied, applied_inner, sums, edges, before, after, full]
        args += history + outers + inners + images + image_inners + ghosts + rims
        outs = []
        if column:
            outs += [outer_shape, inner_shape, side, shape((ch_count, 2, 8, 128))]
        outs += [outer_shape, inner_shape, outer_shape, inner_shape]
        outs += [shape((ch_count, 1, 8, 128))] if last_step else packed
        results = list(
            pl.pallas_call(
                functools.partial(step_kernel, column, last_step),
                out_shape=outs,
                in_specs=[smem, smem] + [vmem] * (len(args) - 2),
                out_specs=[vmem] * len(outs),
                scratch_shapes=[pltpu.VMEM((2, 8, ch_count * ch_dev), jnp.float32)],
                compiler_params=params,
                name="step",
            )(*args)
        )
        if column:
            new = results[:4]
            results = results[4:]
        else:
            new = [applied, applied_inner, sums, edges]
        for store, value in zip((outers, inners, ghosts, rims), new):
            store.append(value)
        history.append(sums)
        image, image_inner, applied, applied_inner = results[:4]
        images.append(image)
        image_inners.append(image_inner)
        payload = results[4:]
    last_sums = exchange(dims, payload[0].reshape(ch_count, 8, 128))[0]
    args = history + [last_sums] + outers + inners
    return tuple(
        pl.pallas_call(
            functools.partial(finish_kernel, 2 * rows_dev),
            out_shape=[outer_shape, inner_shape],
            in_specs=[vmem] * len(args),
            out_specs=[vmem] * 2,
            compiler_params=params,
            name="finish",
        )(*args)
    )


def solution(mesh):
    placed = (
        P(None, "ch", "sec"),
        P(None, ("sec", "ch")),
        P(None, ("sec", "ch"), None),
        P(("sec", "ch")),
        P("ch", None, None, None),
        P(),
        P(),
        P(),
        P(),
    )
    return jax.shard_map(
        functools.partial(per_device, (8, 8, 2, 4)),
        mesh=mesh,
        in_specs=placed,
        out_specs=(P(None, "ch", "sec"), P(None, ("sec", "ch"))),
        check_vma=False,
    )
```

```python
import functools

import jax
import jax.numpy as jnp
from jax import lax
from jax.experimental import pallas as pl
from jax.experimental.pallas import tpu as pltpu
from jax.sharding import PartitionSpec as P

ITERS = 4


inner_radius = 20.0
grid_step = 0.08
time_step = 0.01
stencil_scale = 1.0 / (24.0 * grid_step * grid_step)
taylor_terms = 10
squarings = 7
highest = lax.Precision.HIGHEST


def radial_factor(kind_map, polar_map, laser_field, radius):
    radius_ratio = inner_radius / radius
    dipole_like = radius_ratio * radius_ratio
    quadrupole_like = dipole_like * radius_ratio
    chosen = jnp.sum(
        jnp.where(polar_map[..., None] == jnp.arange(3, dtype=jnp.int32), laser_field, 0.0), axis=-1
    )
    laser_term = chosen[..., None] * radius
    kind_wide = kind_map[..., None]
    return jnp.where(
        kind_wide == 0, dipole_like, jnp.where(kind_wide == 1, quadrupole_like, laser_term)
    )


MESH = pl.DeviceIdType.MESH


def exchange_kernel(dims, bulk, *refs):
    y_size, z_size, c_size, x_size = dims
    if bulk:
        (ghost_in, edge_in, first_in, last_in, outer_in) = refs[:5]
        (sum_out, edge_out, before_out, after_out, full_out) = refs[5:10]
        refs = refs[10:]
    else:
        (ghost_in, sum_out) = refs[:2]
        refs = refs[2:]
    (x_slots, c_slots, z_slots, y_slots) = refs[:4]
    (x_send, x_recv, c_send, c_recv, z_send, z_recv, y_send, y_recv) = refs[4:12]
    if bulk:
        (bulk_send, bulk_recv, side_send, side_recv, edge_send, edge_recv, own_sem) = refs[12:19]
        (cross_send, pass_send, pass_recv, c_land) = refs[19:]
    sec = lax.axis_index("sec")
    x = lax.axis_index("ch")
    c = lax.rem(sec, c_size)
    z = lax.rem(sec // c_size, z_size)
    y = sec // (c_size * z_size)
    sec_size = y_size * z_size * c_size
    rows = ghost_in.shape[1]

    def x_peer(d):
        return {"ch": lax.rem(x + d, x_size)}

    def c_peer(d):
        return {"sec": (y * z_size + z) * c_size + lax.rem(c + d, c_size)}

    def z_peer(d):
        return {"sec": (y * z_size + lax.rem(z + d, z_size)) * c_size + c}

    def y_peer(d):
        return {"sec": (lax.rem(y + d, y_size) * z_size + z) * c_size + c}

    up = {"sec": lax.rem(sec + 1, sec_size)}
    down = {"sec": lax.rem(sec + sec_size - 1, sec_size)}

    greeted = []
    for size, peer in ((x_size, x_peer), (c_size, c_peer), (z_size, z_peer), (y_size, y_peer)):
        greeted += [peer(d) for d in range(1, size)]
    def cross_peer(d):
        return dict(x_peer(d), **c_peer(1))

    if bulk:
        greeted += [up, down]
        greeted += [cross_peer(d) for d in range(1, x_size)]
    barrier = pltpu.get_barrier_semaphore()
    for peer in greeted:
        pl.semaphore_signal(barrier, inc=1, device_id=peer, device_id_type=MESH)
    pl.semaphore_wait(barrier, len(greeted))

    def remote(src, dst, send, recv, peer):
        copy = pltpu.make_async_remote_copy(
            src_ref=src,
            dst_ref=dst,
            send_sem=send,
            recv_sem=recv,
            device_id=peer,
            device_id_type=MESH,
        )
        copy.start()
        return copy

    x_copies = []
    for d in range(1, x_size):
        x_copies.append(
            remote(
                ghost_in.at[lax.rem(x + d, x_size)],
                x_slots.at[x],
                x_send.at[d - 1],
                x_recv.at[d - 1],
                x_peer(d),
            )
        )
    later = []
    if bulk:
        later.append(remote(last_in, before_out, side_send.at[0], side_recv.at[0], up))
        later.append(remote(first_in, after_out, side_send.at[1], side_recv.at[1], down))
        near = []
        for d in range(1, x_size):
            if x_size == 4 and d == 2:
                continue
            near.append(
                remote(
                    outer_in, full_out.at[x], bulk_send.at[d - 1], bulk_recv.at[d - 1], x_peer(d)
                )
            )
        own = pltpu.make_async_copy(outer_in, full_out.at[x], own_sem)
        own.start()
        later.append(own)
    x_slots[x] = ghost_in[x]
    for copy in x_copies:
        copy.wait()

    def total(slots, size):
        value = slots[0]
        for k in range(1, size):
            value = value + slots[k]
        return value

    if bulk:
        c_slots[0] = total(x_slots, x_size)
        c_slots[1] = edge_in[...]
    else:
        c_slots[c] = total(x_slots, x_size)

    def stage(slots, me, size, peer, send, recv):
        copies = []
        for d in sorted(range(1, size), key=lambda d: -min(d, size - d)):
            copies.append(
                remote(slots.at[me], slots.at[me], send.at[d - 1], recv.at[d - 1], peer(d))
            )
        for copy in copies:
            copy.wait()
        return total(slots, size)

    if bulk:
        remote(c_slots.at[1 - c], c_land, c_send.at[0], c_recv.at[0], c_peer(1)).wait()
        z_slots[z] = c_slots[c] + c_land[...]
    else:
        z_slots[z] = stage(c_slots, c, c_size, c_peer, c_send, c_recv)
    y_slots[y] = stage(z_slots, z, z_size, z_peer, z_send, z_recv)
    if bulk:
        for copy in near:
            copy.wait()
        if x_size == 4:
            for half, d, sem in ((0, 1, 1), (1, 3, 3)):
                held = full_out.at[lax.rem(x + x_size - d, x_size), half]
                later.append(remote(held, held, bulk_send.at[sem], bulk_recv.at[sem], x_peer(d)))
    value = stage(y_slots, y, y_size, y_peer, y_send, y_recv)
    if not bulk:
        sum_out[...] = value
        return

    def pass_sums():
        return pltpu.make_async_remote_copy(
            src_ref=sum_out,
            dst_ref=sum_out,
            send_sem=pass_send,
            recv_sem=pass_recv,
            device_id=c_peer(1),
            device_id_type=MESH,
        )

    def edge_from(d):
        place = edge_out.at[lax.rem(x + x_size - d, x_size)]
        return pltpu.make_async_remote_copy(
            src_ref=place,
            dst_ref=place,
            send_sem=edge_send.at[d],
            recv_sem=edge_recv.at[d],
            device_id=cross_peer(d),
            device_id_type=MESH,
        )

    @pl.when(c == 0)
    def _():
        sum_out[...] = value
        copy = pass_sums()
        copy.start()
        copy.wait_send()
        for d in range(x_size):
            edge_from(d).wait_recv()

    @pl.when(c == 1)
    def _():
        edge_out[x] = value
        place = edge_out.at[x]
        copies = []
        across = []
        for d in range(x_size):
            across.append(
                remote(place, place, cross_send.at[d], edge_recv.at[d], cross_peer(d))
            )
            if d:
                copies.append(remote(place, place, edge_send.at[d], edge_recv.at[d], x_peer(d)))
        for copy in across:
            copy.wait_send()
        for copy in copies:
            copy.wait()
        pass_sums().wait_recv()

    for copy in later:
        copy.wait()


def exchange(dims, ghosts, edges=None, first=None, last=None, outer=None):
    bulk = outer is not None
    y_size, z_size, c_size, x_size = dims
    x_count, rows, lanes = ghosts.shape
    vmem = pl.BlockSpec(memory_space=pltpu.VMEM)
    hbm = pl.BlockSpec(memory_space=pl.ANY)
    shape = functools.partial(jax.ShapeDtypeStruct, dtype=jnp.float32)
    outs = [shape((rows, lanes))]
    args = [ghosts]
    width = rows
    if bulk:
        args += [edges, first, last, outer]
        side = edges.shape
        outs += [shape((x_size,) + side), shape(side), shape(side), shape((x_size,) + outer.shape)]
    dma = pltpu.SemaphoreType.DMA
    scratch = [
        pltpu.VMEM((x_size, rows, lanes), jnp.float32),
        pltpu.VMEM((c_size, width, lanes), jnp.float32),
        pltpu.VMEM((z_size, width, lanes), jnp.float32),
        pltpu.VMEM((y_size, width, lanes), jnp.float32),
    ]
    for size in (x_size, c_size, z_size, y_size):
        scratch += [dma((max(size - 1, 1),)), dma((max(size - 1, 1),))]
    if bulk:
        scratch += [dma((x_size,)), dma((x_size,)), dma((2,)), dma((2,))]
        scratch += [dma((x_size,)), dma((x_size,)), dma]
        scratch += [dma((x_size,)), dma, dma, pltpu.VMEM((rows, lanes), jnp.float32)]
    return pl.pallas_call(
        functools.partial(exchange_kernel, dims, bulk),
        out_shape=outs,
        in_specs=[vmem] * len(args),
        out_specs=[vmem] * 4 + [hbm] if bulk else [vmem],
        scratch_shapes=scratch,
        compiler_params=pltpu.CompilerParams(collective_id=1 if bulk else 2, has_side_effects=True),
        name="exchange_bulk" if bulk else "exchange_sums",
    )(*args)


def exact_dot(a, b, dims=((1,), (0,))):
    return lax.dot_general(
        a, b, (dims, ((), ())), precision=highest, preferred_element_type=jnp.float32
    )


def full_sum(value):
    return jnp.sum(jnp.sum(value, axis=0, keepdims=True), axis=1, keepdims=True)


def tile_sum(value):
    return jnp.sum(value.reshape(value.shape[0] // 8, 8, value.shape[1]), axis=0)


def combine(scale, real, imag, terms):
    real, imag = (scale * real, scale * imag)
    for coef_real, coef_imag, other_real, other_imag in terms:
        real = real - (coef_real * other_real - coef_imag * other_imag)
        imag = imag - (coef_real * other_imag + coef_imag * other_real)
    return (real, imag)


def pick(row, k):
    lane = lax.broadcasted_iota(jnp.int32, row.shape, 1)
    return jnp.sum(jnp.where(lane == k, row, 0.0), axis=1, keepdims=True)


def pack(outer, inner, surface, flags, scalars, ghost_out, first_out, last_out, edge_out):
    ch_count = ghost_out.shape[0]
    bs = outer.shape[2]
    blocks = outer.shape[1] // bs
    ghost_out[...] = jnp.zeros_like(ghost_out)
    first_out[...] = jnp.zeros_like(first_out)
    last_out[...] = jnp.zeros_like(last_out)
    row_at = lax.broadcasted_iota(jnp.int32, (8, bs), 0)
    lane_at = lax.broadcasted_iota(jnp.int32, (8, bs), 1)
    wanted = jnp.where(row_at < 2, row_at, jnp.where(row_at < 4, row_at + bs - 4, -1))
    select = (lane_at == wanted).astype(jnp.float32)
    for x in range(2):
        for b in range(blocks):
            rows = exact_dot(select, outer[x, b * bs : (b + 1) * bs, :], ((1,), (1,)))
            for pt in range(2):
                at = pt * blocks + b
                first_out[x, at : at + 1, :] = rows[pt : pt + 1]
                last_out[x, at : at + 1, :] = rows[pt + 2 : pt + 3]
    edge_out[...] = first_out[...] * flags[0]
    for layer in range(2):
        sums = exact_dot(inner, surface[layer])
        for x in range(2):
            for p in range(ch_count):
                for b in range(blocks):
                    at, start = (layer * blocks + b, (p * blocks + b) * bs)
                    ghost_out[p, x, at : at + 1, :] = sums[x : x + 1, start : start + bs]
    put_scalars(scalars, ghost_out, 2 * blocks)


def put_scalars(scalars, ghost_out, at):
    lane = lax.broadcasted_iota(jnp.int32, (1, 128), 1)
    row = jnp.zeros((1, 128), jnp.float32)
    for k, value in enumerate(scalars):
        row = jnp.where(lane == k, value, row)
    for p in range(ghost_out.shape[0]):
        ghost_out[p, 0, at : at + 1, :] = row


def prepare_kernel(flags, outer, inner, surface, ghost_out, first_out, last_out, edge_out):
    value = full_sum(inner[...] * inner[...])
    for x in range(2):
        part = outer[x]
        value = value + full_sum(tile_sum(part * part))
    pack(outer, inner[...], surface, flags, [value], ghost_out, first_out, last_out, edge_out)


def step_kernel(column, last_step, *refs):
    refs = list(refs)
    take = lambda count: [refs.pop(0) for _ in range(count)]
    cols, flags, factor, coef, surface, energies = take(6)
    outer, inner, sums, edges, before, after, full = take(7)
    olds_sums = take(column)
    old_outer, old_inner = (take(column), take(column))
    old_image, old_image_inner = (take(column), take(column))
    old_ghost, old_edge = (take(column), take(column))
    if column:
        new_outer, new_inner, new_ghost, new_edge = take(4)
    else:
        new_outer, new_inner, new_ghost, new_edge = (outer, inner, sums, edges)
    image, image_inner, applied, applied_inner = take(4)
    if last_step:
        (ghost_out,) = take(1)
    else:
        ghost_out, first_out, last_out, edge_out = take(4)
    mixed = take(1)[0]
    bs = outer.shape[2]
    blocks = outer.shape[1] // bs
    slots = coef.shape[1]
    ch_count = edges.shape[0]
    at_row = 2 * blocks

    terms = []
    inverse = None
    if column:
        history = [ref[0, at_row : at_row + 1, :] for ref in olds_sums]
        history.append(sums[0, at_row : at_row + 1, :])
        roots = [lax.rsqrt(pick(history[0], 0) + 1e-06)]
        for k in range(1, column):
            roots.append(lax.rsqrt(pick(history[k + 1], 2 * k + 2) + 1e-06))
        inverse = roots[column - 1]
        for row in range(column):
            scale = roots[row] * roots[row] * inverse
            terms.append(
                (pick(history[column], 2 * row) * scale, pick(history[column], 2 * row + 1) * scale)
            )

    def advance(real, imag, others):
        return combine(
            inverse, real, imag, [t + o for t, o in zip(terms, others)]
        )

    if column:
        real, imag = advance(sums[0], sums[1], [(o[0], o[1]) for o in old_ghost])
        new_ghost[0] = real
        new_ghost[1] = imag
        for p in range(ch_count):
            real, imag = advance(edges[p, 0], edges[p, 1], [(o[p, 0], o[p, 1]) for o in old_edge])
            new_edge[p, 0] = real
            new_edge[p, 1] = imag
        real, imag = advance(
            inner[0:1], inner[1:2], [(o[0:1], o[1:2]) for o in old_inner]
        )
        new_inner[0:1] = real
        new_inner[1:2] = imag
        real, imag = advance(
            energies[...] * inner[0:1],
            energies[...] * inner[1:2],
            [(o[0:1], o[1:2]) for o in old_image_inner],
        )
        image_inner[0:1] = real
        image_inner[1:2] = imag
    else:
        image_inner[...] = energies[...] * inner[...]

    mixed[...] = jnp.zeros_like(mixed)
    for p in range(ch_count):
        for x in range(2):
            for b in range(blocks):
                start = (p * blocks + b) * bs
                zero = new_edge[p, x, b : b + 1, :]
                one = new_edge[p, x, blocks + b : blocks + b + 1, :]
                mixed[0, x : x + 1, start : start + bs] = -16.0 * zero + one
                mixed[1, x : x + 1, start : start + bs] = zero
    added = exact_dot(mixed[0], surface[0], ((1,), (1,)))
    added = added + exact_dot(mixed[1], surface[1], ((1,), (1,)))
    applied_inner[...] = image_inner[...] + stencil_scale * added[0:2]

    row_at = lax.broadcasted_iota(jnp.int32, (8, bs), 0)
    lane_at = lax.broadcasted_iota(jnp.int32, (8, bs), 1)

    def weight(row, lane, value):
        return jnp.where((row_at == row) & (lane_at == lane), value * stencil_scale, 0.0)

    weights = (
        weight(0, 0, 1.0)
        + weight(1, 0, -16.0)
        + weight(1, 1, 1.0)
        + weight(2, bs - 1, -16.0)
        + weight(2, bs - 2, 1.0)
        + weight(3, bs - 1, 1.0)
    )
    zeros = jnp.zeros((4, bs), jnp.float32)
    lane = lax.broadcasted_iota(jnp.int32, (bs, bs), 1)

    def rim(far, near, next0, next1):
        rows = jnp.concatenate([far, near, next0, next1, zeros], axis=0)
        return exact_dot(rows, weights, ((0,), (0,)))

    count = column + 1
    reals = [jnp.zeros((8, bs), jnp.float32) for _ in range(count)]
    imags = [jnp.zeros((8, bs), jnp.float32) for _ in range(count)]
    square = jnp.zeros((8, bs), jnp.float32)
    for b in range(blocks):
        rows = slice(b * bs, (b + 1) * bs)
        product = jnp.zeros((bs, 2 * bs), jnp.float32)
        for s in range(0, slots, 2):
            sides = []
            for t in (s, s + 1):
                col = cols[b, t]
                place = pl.ds(pl.multiple_of(lax.rem(col, blocks) * bs, bs), bs)
                owner = lax.div(col, blocks)
                scale = factor[b, t : t + 1, :]
                sides.append(
                    jnp.concatenate(
                        [full[owner, 0, place, :] * scale, full[owner, 1, place, :] * scale], axis=1
                    )
                )
            left = jnp.concatenate([coef[b, s], coef[b, s + 1]], axis=1)
            product = product + exact_dot(left, jnp.concatenate(sides, axis=0))
        parts = []
        for x in range(2):
            value = outer[x, rows, :]
            m1 = jnp.where(lane >= 1, pltpu.roll(value, 1, 1), 0.0)
            m2 = jnp.where(lane >= 2, pltpu.roll(value, 2, 1), 0.0)
            p1 = jnp.where(lane < bs - 1, pltpu.roll(value, bs - 1, 1), 0.0)
            p2 = jnp.where(lane < bs - 2, pltpu.roll(value, bs - 2, 1), 0.0)
            stencil = stencil_scale * (m2 - 16.0 * m1 + 30.0 * value - 16.0 * p1 + p2)
            sides = rim(
                before[x, b : b + 1, :] * flags[1],
                before[x, blocks + b : blocks + b + 1, :] * flags[1],
                after[x, b : b + 1, :] * flags[2],
                after[x, blocks + b : blocks + b + 1, :] * flags[2],
            )
            parts.append(stencil + sides + product[:, x * bs : (x + 1) * bs])
        vector = [outer[0, rows, :], outer[1, rows, :]]
        if column:
            parts = advance(
                parts[0], parts[1], [(o[0, rows, :], o[1, rows, :]) for o in old_image]
            )
            vector = advance(
                vector[0], vector[1], [(o[0, rows, :], o[1, rows, :]) for o in old_outer]
            )
            for x in range(2):
                new_outer[x, rows, :] = vector[x]
        result = []
        none = jnp.zeros((1, bs), jnp.float32)
        for x in range(2):
            if not last_step:
                image[x, rows, :] = parts[x]
            value = parts[x] + rim(
                new_ghost[x, blocks + b : blocks + b + 1, :] * flags[0],
                new_ghost[x, b : b + 1, :] * flags[0],
                none,
                none,
            )
            if not last_step:
                applied[x, rows, :] = value
            result.append(value)
        for k in range(count):
            if k < column:
                own = [old_outer[k][x, rows, :] for x in range(2)]
            else:
                own = vector
            reals[k] = reals[k] + tile_sum(own[0] * result[0] + own[1] * result[1])
            imags[k] = imags[k] + tile_sum(own[0] * result[1] - own[1] * result[0])
        square = square + tile_sum(vector[0] * vector[0] + vector[1] * vector[1])

    scalars = []
    w_real, w_imag = (applied_inner[0:1], applied_inner[1:2])
    for k in range(count):
        ref = old_inner[k] if k < column else new_inner
        u_real, u_imag = (ref[0:1], ref[1:2])
        scalars.append(full_sum(reals[k]) + full_sum(u_real * w_real + u_imag * w_imag))
        scalars.append(full_sum(imags[k]) + full_sum(u_real * w_imag - u_imag * w_real))
    scalars.append(full_sum(square) + full_sum(new_inner[...] * new_inner[...]))
    if last_step:
        ghost_out[...] = jnp.zeros_like(ghost_out)
        put_scalars(scalars, ghost_out, at_row)
    else:
        pack(
            applied,
            applied_inner[...],
            surface,
            flags,
            scalars,
            ghost_out,
            first_out,
            last_out,
            edge_out,
        )


def small_product(a, b):
    value = a[:, 0:1] * b[0:1, :]
    for k in range(1, 2 * ITERS):
        value = value + a[:, k : k + 1] * b[k : k + 1, :]
    return value


def finish_kernel(at_row, *refs):
    history = [ref[0, at_row : at_row + 1, :] for ref in refs[:ITERS]]
    history.append(refs[ITERS][at_row : at_row + 1, :])
    outers, inners = (refs[ITERS + 1 : 2 * ITERS + 1], refs[2 * ITERS + 1 : 3 * ITERS + 1])
    outer_out, inner_out = refs[3 * ITERS + 1 :]
    squares = [pick(history[0], 0) + 1e-06]
    for k in range(1, ITERS):
        squares.append(pick(history[k + 1], 2 * k + 2) + 1e-06)
    roots = [lax.rsqrt(value) for value in squares]
    row_at = lax.broadcasted_iota(jnp.int32, (2 * ITERS, 128), 0)
    lane_at = lax.broadcasted_iota(jnp.int32, (2 * ITERS, 128), 1)
    matrix = jnp.zeros((2 * ITERS, 128), jnp.float32)

    def put(value, i, j):
        return jnp.where((row_at == i) & (lane_at == j), value, matrix)

    for j in range(ITERS):
        for i in range(min(j + 2, ITERS)):
            if i <= j:
                scale = roots[i] * roots[j] * time_step
                real = pick(history[j + 1], 2 * i) * scale
                imag = pick(history[j + 1], 2 * i + 1) * scale
                matrix = put(imag, i, j)
                matrix = put(imag, i + ITERS, j + ITERS)
            else:
                real = jnp.sqrt(squares[i]) * time_step
            matrix = put(real, i, j + ITERS)
            matrix = put(-real, i + ITERS, j)
    matrix = matrix * (1.0 / 2.0**squarings)
    identity = jnp.where(row_at == lane_at, 1.0, 0.0)
    series = identity
    for degree in range(taylor_terms, 0, -1):
        series = identity + small_product(matrix, series) * (1.0 / degree)
    for repeat in range(squarings):
        series = small_product(series, series)
    terms = []
    start_norm = jnp.sqrt(squares[0])
    for j in range(ITERS):
        scale = start_norm * roots[j]
        terms.append((series[j : j + 1, 0:1] * scale, series[j + ITERS : j + ITERS + 1, 0:1] * scale))

    def total(values):
        real, imag = (0.0, 0.0)
        for (part_real, part_imag), (value_real, value_imag) in zip(terms, values):
            real = real + (part_real * value_real - part_imag * value_imag)
            imag = imag + (part_real * value_imag + part_imag * value_real)
        return (real, imag)

    inner_out[0:1], inner_out[1:2] = total([(ref[0:1], ref[1:2]) for ref in inners])
    bs = outer_out.shape[2]
    for b in range(outer_out.shape[1] // bs):
        rows = slice(b * bs, (b + 1) * bs)
        real, imag = total([(ref[0, rows, :], ref[1, rows, :]) for ref in outers])
        outer_out[0, rows, :] = real
        outer_out[1, rows, :] = imag


def per_device(
    dims,
    outer_wave,
    inner_wave,
    surface,
    energies,
    coefficients,
    block_cols,
    block_kind,
    polarisation,
    laser_field,
):
    sec_index = lax.axis_index("sec")
    ch_index = lax.axis_index("ch")
    ch_count = lax.axis_size("ch")
    ch_dev = outer_wave.shape[1]
    rad_dev = outer_wave.shape[2]
    block_size = coefficients.shape[2]
    rows_dev = coefficients.shape[0]
    positions = sec_index * rad_dev + jnp.arange(rad_dev, dtype=jnp.int32)
    radius = inner_radius + (positions + 1).astype(jnp.float32) * grid_step
    first_sector = (sec_index == 0).astype(jnp.float32)
    last_sector = (sec_index == lax.axis_size("sec") - 1).astype(jnp.float32)
    local_cols = lax.dynamic_slice_in_dim(block_cols, ch_index * rows_dev, rows_dev, 0)
    local_kind = lax.dynamic_slice_in_dim(block_kind, ch_index * rows_dev, rows_dev, 0)
    local_polar = lax.dynamic_slice_in_dim(polarisation, ch_index * rows_dev, rows_dev, 0)
    local_factor = radial_factor(local_kind, local_polar, laser_field, radius)
    flags = jnp.stack([first_sector, 1.0 - first_sector, 1.0 - last_sector])
    shape = functools.partial(jax.ShapeDtypeStruct, dtype=jnp.float32)
    vmem = pl.BlockSpec(memory_space=pltpu.VMEM)
    smem = pl.BlockSpec(memory_space=pltpu.SMEM)
    params = pltpu.CompilerParams(vmem_limit_bytes=56 * 1024 * 1024)
    side = shape((2, 8, 128))
    packed = [shape((ch_count, 2, 8, 128)), side, side, side]
    outer_shape, inner_shape = (shape(outer_wave.shape), shape(inner_wave.shape))

    def swap(vector, payload):
        ghost_part, first, last, edge = [value.reshape(-1, 16, 128) for value in payload]
        sums, edges, before, after, full = exchange(
            dims, ghost_part, edge[0], first[0], last[0], vector
        )
        return (
            sums.reshape(2, 8, 128),
            edges.reshape(ch_count, 2, 8, 128),
            before.reshape(2, 8, 128),
            after.reshape(2, 8, 128),
            full,
        )

    payload = pl.pallas_call(
        prepare_kernel,
        out_shape=packed,
        in_specs=[smem] + [vmem] * 3,
        out_specs=[vmem] * 4,
        compiler_params=params,
        name="prepare",
    )(flags, outer_wave, inner_wave, surface)
    applied, applied_inner = (outer_wave, inner_wave)
    history, outers, inners, images, image_inners, ghosts, rims = ([], [], [], [], [], [], [])
    for column in range(ITERS):
        last_step = column + 1 == ITERS
        sums, edges, before, after, full = swap(applied, payload)
        args = [local_cols, flags, local_factor, coefficients, surface, energies[None]]
        args += [applied, applied_inner, sums, edges, before, after, full]
        args += history + outers + inners + images + image_inners + ghosts + rims
        outs = []
        if column:
            outs += [outer_shape, inner_shape, side, shape((ch_count, 2, 8, 128))]
        outs += [outer_shape, inner_shape, outer_shape, inner_shape]
        outs += [shape((ch_count, 1, 8, 128))] if last_step else packed
        results = list(
            pl.pallas_call(
                functools.partial(step_kernel, column, last_step),
                out_shape=outs,
                in_specs=[smem, smem] + [vmem] * (len(args) - 2),
                out_specs=[vmem] * len(outs),
                scratch_shapes=[pltpu.VMEM((2, 8, ch_count * ch_dev), jnp.float32)],
                compiler_params=params,
                name="step",
            )(*args)
        )
        if column:
            new = results[:4]
            results = results[4:]
        else:
            new = [applied, applied_inner, sums, edges]
        for store, value in zip((outers, inners, ghosts, rims), new):
            store.append(value)
        history.append(sums)
        image, image_inner, applied, applied_inner = results[:4]
        images.append(image)
        image_inners.append(image_inner)
        payload = results[4:]
    last_sums = exchange(dims, payload[0].reshape(ch_count, 8, 128))[0]
    args = history + [last_sums] + outers + inners
    return tuple(
        pl.pallas_call(
            functools.partial(finish_kernel, 2 * rows_dev),
            out_shape=[outer_shape, inner_shape],
            in_specs=[vmem] * len(args),
            out_specs=[vmem] * 2,
            compiler_params=params,
            name="finish",
        )(*args)
    )


def solution(mesh):
    placed = (
        P(None, "ch", "sec"),
        P(None, ("sec", "ch")),
        P(None, ("sec", "ch"), None),
        P(("sec", "ch")),
        P("ch", None, None, None),
        P(),
        P(),
        P(),
        P(),
    )
    return jax.shard_map(
        functools.partial(per_device, (8, 8, 2, 4)),
        mesh=mesh,
        in_specs=placed,
        out_specs=(P(None, "ch", "sec"), P(None, ("sec", "ch"))),
        check_vma=False,
    )
```
